32 devices in a mesh: groups: 2 (over y), gx: 16 (over z, x, core).
Axes of the slice: x: 2, y: 2, z: 4, core: 2. Of those that a mesh axis runs over, the one named last changes fastest.
Arguments:
- initial: float32 [20, 4, 256, 1024], P('groups', None, 'gx'), parts along dimension 0, may hold values from -6 to 6
- background: float32 [20, 4, 256, 1024], P('groups', None, 'gx'), parts along dimension 0, may hold values from -6.5 to 6.5
- mixing: float32 [40, 40], replicated, may hold values from -1 to 1
- diffusion: float32 [10, 4], replicated, may hold values from 0.03 to 0.2
- advection: float32 [2, 10, 4], replicated, may hold values from -0.1 to 0.1
- obs_values: float32 [4, 4096], P('groups', 'gx'), parts along dimension 0, may hold values from -6 to 6
- obs_weight: float32 [2, 4096], P('groups', 'gx'), parts along dimension 0, may hold values from 0.5 to 4
- interp_weights: float32 [8, 4096], P('groups', 'gx'), parts along dimension 0, may hold values from 0.1 to 1
- stencil_index: int32 [8, 4096], P('groups', 'gx'), parts along dimension 0, may hold values from 0 to 655359, as said below
- station_tile: int32 [4096, 2], P('gx', 'groups'), parts along dimension 1, may hold values from 0 to 15; in each aligned block of 256 rows (0 to 255, 256 to 511, ...) at most 24 rows name the same one
- counts: int32 [2, 16], P('groups', 'gx'), parts along dimension 0, may hold values from 1 to 256, 3072 in all within a row
Outputs:
- gradient: float32 [20, 4, 256, 1024], P('groups', None, 'gx'), parts along dimension 0
The draws below stay inside these ranges and needn't reach their ends.
There are 2 independent parts, one for each index of `groups`. The reference program is written for one: setup_inputs(seed, part) draws one part's arguments, and reference() takes and returns one part's arrays. A program takes and returns all parts, laid end to end along the dimension named above; an argument that names none is the same for every part. Nothing has to cross between parts.
Inputs may be any that keep to these rules, and one draw needn't show every extreme that they name: `station_tile`: within the rows of one device, no tile is named more than 24 times; some tile is named exactly 24 times in some or all devices' rows. Live observations of a tile occupy its first counts slots; some tile has 256. `stencil_index`: each column holds four cells of one channel of the owner tile, a cell being (channel * 16 + row) * 1024 + column: (row, column), (row, column + 1), (row + 1, column), (row + 1, column + 1) in that order.
All inputs are finite; a program needn't handle non-finite values. No bound on the sum of `counts` on one device may be relied on, other than what follows from the above.
Results may differ from the reference program's by a relative error of at most 0.00014.
Values sent between devices are 32-bit elements; how exact they have to be, the bound alone decides.
A program may use at most 64 MiB of HBM per device.

```python
import math
import jax
import jax.numpy as jnp
import numpy as np
from jax import lax

F = 10
L = 4
NY = 1024
CX = 16
OBS_DEV = 256
NX = 256
OBS_TOTAL = 4096
CAP = 24
N_GX = 16


def base_state(key):
    state_key = jax.random.fold_in(key, 11)
    raw = jnp.clip(jax.random.normal(state_key, (F, L, NX, NY), jnp.float32), -6.0, 6.0)
    return raw


def draw_initial(key, part):
    return base_state(key).astype(jnp.float32)


def draw_background(key, part):
    step_key = jax.random.fold_in(key, 12)
    increment = 0.1 * jnp.clip(jax.random.normal(step_key, (F, L, NX, NY), jnp.float32), -4.0, 4.0)
    return (base_state(key) + increment).astype(jnp.float32)


def draw_stencil_index(key, part):
    keys = jax.random.split(key, 3)
    channel = jax.random.randint(keys[0], (OBS_TOTAL,), 0, F * L)
    row_start = jax.random.randint(keys[1], (OBS_TOTAL,), 0, CX - 1)
    col_start = jax.random.randint(keys[2], (OBS_TOTAL,), 0, NY - 1)
    base_cell = (channel * CX + row_start) * NY + col_start
    offsets = jnp.array([0, 1, NY, NY + 1], jnp.int32)
    return (base_cell[None, :] + offsets[:, None]).astype(jnp.int32)


def block_levels(stream_key, dims, pieces, low, top_value):
    factor_of = 1.0
    for axis_at, shards_of in pieces:
        draws = jax.random.uniform(jax.random.fold_in(jax.random.fold_in(stream_key, 6), axis_at), (shards_of,), jnp.float32, low / len(pieces), top_value / len(pieces))
        factor_of = factor_of * jnp.repeat(jnp.exp(draws), dims[axis_at] // shards_of).reshape((-1,) + (1,) * (len(dims) - 1 - axis_at))
    return factor_of


def length_profile(amount, total, limit, lean):
    loads = [(1 << 20) // math.isqrt(standing ** lean) + 1 for standing in range(2, amount + 1)]
    spare, given = total - limit - (amount - 1), [1] * (amount - 1)
    while spare > 0:
        free = [i for i in range(amount - 1) if given[i] < limit]
        mass, budget = sum([loads[i] for i in free]), spare
        for i in free:
            extra = min(limit - given[i], max(1, budget * loads[i] // mass), spare)
            given[i] = given[i] + extra
            spare = spare - extra
    return np.array([limit] + given)


def uneven_parts(key, amount, total, most, skew):
    if amount == 2:
        one = jax.random.randint(key, (), max(1, total - most), min(most, total - 1) + 1)
        return jnp.stack([one, total - one])
    sizes = jnp.asarray(length_profile(amount, total, most, skew), jnp.int32)
    twos = (amount - 1) // 2
    source_of, sink = sizes[1:1 + 2 * twos:2], sizes[2:2 + 2 * twos:2]
    slack = jnp.minimum(source_of - 1, most - sink)
    passed = jax.random.randint(jax.random.fold_in(key, 1), (twos,), 0, 1 << 20) % (slack + 1)
    sizes = sizes.at[1:1 + 2 * twos:2].set(source_of - passed).at[2:2 + 2 * twos:2].set(sink + passed)
    return sizes[jax.random.permutation(jax.random.fold_in(key, 2), amount)]


def deal_out(stream_key, own, number, rows, count, top, bound, lean):
    sequence = jax.random.permutation(stream_key, count)
    crowded, usual = shares(count, rows * top, bound, lean, True), shares(count, rows * top, bound, lean, False)
    places = jnp.arange(count)

    def named(lengths, turn):
        used = int((lengths > 0).sum())
        fixed = max(1, used // 4)
        moved = fixed + (places - fixed + turn * (used - fixed)) % max(1, count - fixed)
        return jnp.zeros((count,), jnp.int32).at[sequence[jnp.where(places < fixed, places, moved)]].set(jnp.asarray(lengths, jnp.int32))

    lengths = jnp.where(number % 4 == 0, named(crowded, number // 4), named(usual, number - number // 4 - 1))
    mixed = jax.random.permutation(jax.random.fold_in(own, 3), count)
    giver, receiver = mixed[0:count // 2 * 2:2], mixed[1:count // 2 * 2:2]
    room = jnp.minimum(lengths[giver] - 1, bound - lengths[receiver]) // 2
    room = jnp.where((giver == sequence[0]) | (receiver == sequence[0]) | (lengths[receiver] == 0), 0, jnp.maximum(room, 0))
    moved = jax.random.randint(jax.random.fold_in(own, 4), (count // 2,), 0, 1 << 20) % (room + 1)
    lengths = lengths.at[giver].add(-moved).at[receiver].add(moved)
    members = jnp.searchsorted(jnp.cumsum(lengths), jnp.arange(rows * top), side="right").astype(jnp.int32)
    grid = members.reshape(top, rows).T
    grid = grid[jax.random.permutation(jax.random.fold_in(own, 1), rows)]
    turn = jax.random.randint(jax.random.fold_in(own, 2), (rows, 1), 0, top)
    return jnp.take_along_axis(grid, (jnp.arange(top)[None, :] + turn) % top, axis=1)


def shares(amount, total, limit, lean, full):
    weights = [(1 << 20) // math.isqrt(rank ** lean) + 1 for rank in range(1, amount + 1)]
    largest = limit if full else min(limit, max(-(-total // amount), total * weights[0] // sum(weights)))
    least = 1 if total - largest >= amount - 1 else 0
    given, spare = [largest] + [least] * (amount - 1), total - largest - least * (amount - 1)
    while spare > 0:
        free = [i for i in range(1, amount) if given[i] < largest] or [i for i in range(1, amount) if given[i] < limit]
        pool, left = sum([weights[i] for i in free]), spare
        for i in free:
            extra = min(limit - given[i], max(1, left * weights[i] // pool), spare)
            given[i] = given[i] + extra
            spare = spare - extra
    return np.array(given)


def bell_draw(stream_key, shape, scale, limit, pieces=(), kind=jnp.bfloat16):
    result = jax.random.normal(stream_key, shape, jnp.float32) * scale
    if len(pieces) > 0:
        result = block_levels(stream_key, shape, pieces, -0.22, 0.18) * result
    return jnp.clip(result, min=-limit, max=limit).astype(kind)


def setup_inputs(seed: int = 0, part: int = 0) -> dict:
    key_list = jax.random.split(jax.random.key(seed), 12)
    own_keys = jax.random.split(jax.random.fold_in(key_list[11], part), 12)
    initial = draw_initial(jax.random.fold_in(jax.random.fold_in(key_list[11], part), 71), part)
    background = draw_background(jax.random.fold_in(jax.random.fold_in(key_list[11], part), 71), part)
    mixing = bell_draw(key_list[2], (F * L, F * L), (F * L) ** -0.5, 1.0, (), jnp.float32)
    diffusion = jnp.clip(jnp.exp(jax.random.uniform(key_list[3], (F, L), jnp.float32, math.log(0.03), math.log(0.2))), 0.03, 0.2)
    advection = jnp.clip(jax.random.uniform(key_list[4], (2, F, L), jnp.float32, -0.1, 0.1), -0.1, 0.1)
    obs_values = bell_draw(own_keys[5], (2, OBS_TOTAL), 1.0, 6.0, ((1, 16),), jnp.float32)
    obs_weight = jnp.clip(jnp.exp(math.log(4.0) - 2.0794415 * jax.random.uniform(own_keys[6], (1, OBS_TOTAL), jnp.float32) ** block_levels(own_keys[6], (1, OBS_TOTAL), ((1, 16),), -0.2, 0.2)), 0.5, 4.0)
    interp_weights = jnp.clip(0.1 + 0.9 * jax.random.uniform(own_keys[7], (4, OBS_TOTAL), jnp.float32) ** block_levels(own_keys[7], (4, OBS_TOTAL), ((1, 16),), -0.2, 0.2), 0.1, 1.0)
    stencil_index = draw_stencil_index(jax.random.fold_in(jax.random.fold_in(key_list[11], part), 71), part)
    station_tile_keys = jax.random.split(jax.random.fold_in(own_keys[9], 1), OBS_TOTAL // OBS_DEV)
    station_tile_turns = jax.random.permutation(jax.random.fold_in(own_keys[9], 3), OBS_TOTAL // OBS_DEV)
    station_tile = jax.vmap(lambda own, number: deal_out(jax.random.fold_in(own_keys[9], 2), own, number, OBS_DEV, N_GX, 1, CAP, 2))(station_tile_keys, station_tile_turns).reshape((OBS_TOTAL, 1))
    counts = jax.vmap(lambda own: uneven_parts(own, N_GX, N_GX * OBS_DEV * 3 // 4, OBS_DEV, 2))(jax.random.split(own_keys[10], 1)).reshape((1, N_GX)).astype(jnp.int32)
    return dict(initial=initial, background=background, mixing=mixing, diffusion=diffusion, advection=advection, obs_values=obs_values, obs_weight=obs_weight, interp_weights=interp_weights, stencil_index=stencil_index, station_tile=station_tile, counts=counts)


def tendency(padded, diffuse_rate, drift_x, drift_y):
    centre_cells = padded[:, 1:-1]
    north_side = padded[:, 2:]
    south_side = padded[:, :-2]
    widened = jnp.pad(centre_cells, ((0, 0), (0, 0), (1, 1)))
    east_side = widened[:, :, 2:]
    west_side = widened[:, :, :-2]
    return (diffuse_rate * (north_side + south_side + east_side + west_side - 4.0 * centre_cells)
            + drift_x * (north_side - south_side) + drift_y * (east_side - west_side))


def reference(initial, background, mixing, diffusion, advection, obs_values, obs_weight, interp_weights, stencil_index, station_tile, counts):
    channels = F * L
    start_state = initial.reshape(channels, NX, NY)
    diffuse_rate = diffusion.reshape(channels, 1, 1)
    drift_x = advection[0].reshape(channels, 1, 1)
    drift_y = advection[1].reshape(channels, 1, 1)

    def advance(state):
        padded = jnp.pad(state, ((0, 0), (1, 1), (0, 0)))
        mixed = jnp.einsum("cd,dxy->cxy", mixing, jnp.tanh(state), precision=lax.Precision.HIGHEST)
        return state + tendency(padded, diffuse_rate, drift_x, drift_y) + mixed

    def retreat(cotangent, state):
        padded = jnp.pad(cotangent, ((0, 0), (1, 1), (0, 0)))
        spread = tendency(padded, diffuse_rate, -drift_x, -drift_y)
        back_mix = jnp.einsum("cd,cxy->dxy", mixing, cotangent, precision=lax.Precision.HIGHEST)
        return cotangent + spread + (1.0 - jnp.tanh(state) ** 2) * back_mix

    state_one = advance(start_state)
    state_two = advance(state_one)
    tile_of = station_tile[:, 0]
    channel = stencil_index // (CX * NY)
    remainder = stencil_index % (CX * NY)
    global_cell = (channel * (NX * NY) + tile_of[None, :] * (CX * NY) + remainder).astype(jnp.int32)
    order = jnp.arange(OBS_TOTAL, dtype=jnp.int32)
    alive_mask = (order % OBS_DEV < counts[0, order // OBS_DEV]).astype(jnp.float32)
    weight = obs_weight[0] * alive_mask

    def forcing_at(state, observed):
        flat_state = state.reshape(-1)
        samples = flat_state[global_cell]
        misfit = weight * (jnp.sum(interp_weights * samples, 0) - observed)
        forcing = jnp.zeros((channels * NX * NY,), jnp.float32)
        forcing = forcing.at[global_cell.reshape(-1)].add((misfit[None, :] * interp_weights).reshape(-1))
        return forcing.reshape(channels, NX, NY)

    cot_two = forcing_at(state_two, obs_values[1])
    cot_one = retreat(cot_two, state_one) + forcing_at(state_one, obs_values[0])
    cot_zero = retreat(cot_one, start_state)
    gradient = (start_state - background.reshape(channels, NX, NY)) + cot_zero
    return gradient.reshape(F, L, NX, NY)
```

```python
import functools
import jax
import jax.numpy as jnp
from jax import lax
from jax.experimental import pallas as pl
from jax.experimental.pallas import tpu as pltpu
from jax.sharding import PartitionSpec as P

MESH = pl.DeviceIdType.MESH
WIN = 256


def fdot(a, b, dims):
    return lax.dot_general(a, b, (dims, ((), ())), preferred_element_type=jnp.float32)


def split3(v):
    hi = v.astype(jnp.bfloat16)
    rest = v - hi.astype(jnp.float32)
    mid = rest.astype(jnp.bfloat16)
    lo = (rest - mid.astype(jnp.float32)).astype(jnp.bfloat16)
    return hi, mid, lo


def widen_mix(m):
    hi = m.astype(jnp.bfloat16)
    lo = (m - hi.astype(jnp.float32)).astype(jnp.bfloat16)
    return jnp.concatenate([hi, hi, lo], axis=1)


def mix_rows(wide, v):
    hi = v.astype(jnp.bfloat16)
    lo = (v - hi.astype(jnp.float32)).astype(jnp.bfloat16)
    return fdot(wide, jnp.concatenate([hi, lo, hi], axis=0), ((1,), (0,)))


def shifts(v):
    cols = v.shape[1]
    lane = lax.broadcasted_iota(jnp.int32, v.shape, 1)
    east = jnp.where(lane == cols - 1, 0.0, pltpu.roll(v, cols - 1, 1))
    west = jnp.where(lane == 0, 0.0, pltpu.roll(v, 1, 1))
    return east, west


def step_rows(centre, above, below, coef):
    east, west = shifts(centre)
    return (
        coef[0] * centre + coef[1] * above + coef[2] * below + coef[3] * east + coef[4] * west
    )


def coef_columns(coef_ref, sign):
    c, a, b = coef_ref[:, 0:1], sign * coef_ref[:, 1:2], sign * coef_ref[:, 2:3]
    return 1.0 - 4.0 * c, c + a, c - a, c + b, c - b


def route_kernel(
    tiles, cap, vals, wts, interp, cells, target, count, u0, recv, halo,
    send, send_sem, recv_sem, halo_send, halo_recv,
):
    me = lax.axis_index("gx")
    rows = u0.shape[1]
    barrier = pltpu.get_barrier_semaphore()

    def greet(d, _):
        pl.semaphore_signal(
            barrier, inc=1, device_id={"gx": lax.rem(me + d, tiles)}, device_id_type=MESH
        )
        return 0

    lax.fori_loop(1, tiles, greet, 0)
    held = target.shape[1]
    slots = tiles * cap
    names = target[...]
    match = (lax.broadcasted_iota(jnp.int32, (tiles, held), 0) == names).astype(jnp.float32)
    before = (
        lax.broadcasted_iota(jnp.int32, (held, held), 0)
        < lax.broadcasted_iota(jnp.int32, (held, held), 1)
    ).astype(jnp.bfloat16)
    ranks = fdot(match.astype(jnp.bfloat16), before, ((1,), (0,)))
    rank = jnp.sum(match * ranks, axis=0, keepdims=True).astype(jnp.int32)
    position = names * cap + rank
    hot = (lax.broadcasted_iota(jnp.int32, (slots, held), 0) == position).astype(jnp.float32)
    hot = hot.astype(jnp.bfloat16)
    live = lax.broadcasted_iota(jnp.int32, (1, held), 1) < count[0, 0]
    weight = jnp.where(live, wts[...], 0.0)
    recs = jnp.concatenate(
        [vals[...], weight, interp[...], cells[0:1, :].astype(jnp.float32),
         jnp.zeros((120, held), jnp.float32)], axis=0)
    hi, mid, lo = split3(recs)
    nt = ((1,), (1,))
    placed = fdot(hot, hi, nt) + fdot(hot, mid, nt) + fdot(hot, lo, nt)
    send[...] = placed.reshape(tiles, cap, 128)
    pl.semaphore_wait(barrier, tiles - 1)

    def edge(up, k):
        if up:
            src, dst, to = rows - 2 + k, k, me + 1
        else:
            src, dst, to = k, 2 + k, me - 1
        return pltpu.make_async_remote_copy(
            src_ref=u0.at[:, src, :],
            dst_ref=halo.at[dst],
            send_sem=halo_send.at[dst],
            recv_sem=halo_recv.at[dst],
            device_id={"gx": to},
            device_id_type=MESH,
        )

    def parcel(d):
        to = lax.rem(me + d, tiles)
        return pltpu.make_async_remote_copy(
            src_ref=send.at[to],
            dst_ref=recv.at[me],
            send_sem=send_sem.at[d],
            recv_sem=recv_sem.at[d],
            device_id={"gx": to},
            device_id_type=MESH,
        )

    def arrived(d):
        source = lax.rem(me + tiles - d, tiles)
        return pltpu.make_async_remote_copy(
            src_ref=send.at[source],
            dst_ref=recv.at[source],
            send_sem=send_sem.at[d],
            recv_sem=recv_sem.at[d],
            device_id={"gx": source},
            device_id_type=MESH,
        )

    def start(d, _):
        parcel(d).start()
        return 0

    def finish(d, _):
        parcel(d).wait_send()
        arrived(d).wait_recv()
        return 0

    lax.fori_loop(1, tiles, start, 0)

    @pl.when(me < tiles - 1)
    def _():
        edge(True, 1).start()
        edge(True, 0).start()

    @pl.when(me > 0)
    def _():
        edge(False, 0).start()
        edge(False, 1).start()

    recv[me] = send[me]
    lax.fori_loop(1, tiles, finish, 0)

    @pl.when(me < tiles - 1)
    def _():
        for k in range(2):
            edge(True, k).wait_send()
            edge(False, k).wait_recv()

    @pl.when(me > 0)
    def _():
        for k in range(2):
            edge(False, k).wait_send()
            edge(True, k).wait_recv()


def window_weights(cell, weights, rows, cols):
    column = cell - jnp.floor(cell * (1.0 / cols)) * cols
    block = jnp.minimum(jnp.floor(column * (1.0 / 128)), float(cols // 128 - 2))
    local = column - 128.0 * block
    lane = lax.broadcasted_iota(jnp.int32, (cell.shape[0], WIN), 1).astype(jnp.float32)
    left, right = lane == local, lane == local + 1.0
    top = jnp.where(left, weights[0], 0.0) + jnp.where(right, weights[1], 0.0)
    low = jnp.where(left, weights[2], 0.0) + jnp.where(right, weights[3], 0.0)
    return top, low


def cell_rows(cell, rows, cols):
    chan = jnp.floor(cell * (1.0 / (rows * cols)))
    rest = cell - chan * (rows * cols)
    line = jnp.floor(rest * (1.0 / cols))
    column = rest - line * cols
    block = jnp.minimum(jnp.floor(column * (1.0 / 128)), float(cols // 128 - 2)) * 128.0
    zero = jnp.zeros_like(cell)
    return jnp.concatenate([line, chan, block] + [zero] * 5, axis=0).astype(jnp.int32)


def forward_kernel(
    tiles, u0, halo, recv, mixing, coef, q1, packed,
    su0, su1, su2, sq1, top_rows, low_rows, place_v, place_s, in_sem, out_sem, place_sem,
):
    me = lax.axis_index("gx")
    chans, rows, cols = u0.shape
    loads = []
    for r in range(rows + 4):
        if 2 <= r < rows + 2:
            source = u0.at[:, r - 2, :]
        else:
            source = halo.at[r if r < 2 else r - rows]
        loads.append(pltpu.make_async_copy(source, su0.at[r], in_sem.at[r]))
    for copy in loads:
        copy.start()
    records = recv[...].reshape(recv.shape[0] * recv.shape[1], recv.shape[2])
    count = records.shape[0]
    turned = records.T
    place_v[...] = cell_rows(turned[7:8, :], rows, cols)
    placing = pltpu.make_async_copy(place_v, place_s, place_sem)
    placing.start()
    wide = widen_mix(mixing[...])
    coefs = coef_columns(coef, 1.0)
    loads[0].wait()
    loads[1].wait()
    loads[rows + 2].wait()
    loads[rows + 3].wait()

    @pl.when(me == 0)
    def _():
        su0[0:2] = jnp.zeros((2, chans, cols), jnp.float32)

    @pl.when(me == tiles - 1)
    def _():
        su0[rows + 2:rows + 4] = jnp.zeros((2, chans, cols), jnp.float32)

    for r in range(2, rows + 2):
        loads[r].wait()
    stores = lambda i: pltpu.make_async_copy(sq1.at[i], q1.at[i], out_sem.at[i])

    def first(i, _):
        centre = su0[i + 1]
        out = step_rows(centre, su0[i + 2], su0[i], coefs) + mix_rows(wide, jnp.tanh(centre))
        su1[i] = out
        return 0

    lax.fori_loop(0, rows + 2, first, 0)

    @pl.when(me == 0)
    def _():
        su1[0] = jnp.zeros((chans, cols), jnp.float32)

    @pl.when(me == tiles - 1)
    def _():
        su1[rows + 1] = jnp.zeros((chans, cols), jnp.float32)

    def second(i, _):
        centre = su1[i + 1]
        th = jnp.tanh(centre)
        sq1[i + 1] = 1.0 - th * th
        stores(i + 1).start()
        su2[i] = step_rows(centre, su1[i + 2], su1[i], coefs) + mix_rows(wide, th)
        return 0

    for i in (0, rows + 1):
        th = jnp.tanh(su1[i])
        sq1[i] = 1.0 - th * th
        stores(i).start()
    lax.fori_loop(0, rows, second, 0)
    placing.wait()
    column = lambda k: records[:, k:k + 1]
    top, low = window_weights(column(7), [column(3 + k) for k in range(4)], rows, cols)
    results = []
    for which, (state, base) in enumerate(((su1, 1), (su2, 0))):

        def gather(j8, _):
            for k in range(8):
                j = j8 * 8 + k
                line, chan = place_s[0, j] + base, place_s[1, j]
                block = pl.multiple_of(place_s[2, j], 128)
                top_rows[pl.ds(j, 1), :] = state[line, pl.ds(chan, 1), pl.ds(block, WIN)]
                low_rows[pl.ds(j, 1), :] = state[line + 1, pl.ds(chan, 1), pl.ds(block, WIN)]
            return 0

        lax.fori_loop(0, count // 8, gather, 0)
        sample = jnp.sum(top_rows[...] * top + low_rows[...] * low, axis=1, keepdims=True)
        results.append(column(2) * (sample - column(which)))
    lane = lax.broadcasted_iota(jnp.int32, records.shape, 1)
    merged = jnp.where(lane == 0, results[0], jnp.where(lane == 1, results[1], records))
    packed[...] = merged.T[0:8, :]
    for i in range(rows + 2):
        stores(i).wait()


def share_kernel(tiles, mine, near, send_sem, recv_sem):
    me = lax.axis_index("gx")
    barrier = pltpu.get_barrier_semaphore()

    def copy(k):
        return pltpu.make_async_remote_copy(
            src_ref=mine, dst_ref=near.at[k], send_sem=send_sem.at[k], recv_sem=recv_sem.at[k],
            device_id={"gx": me + 1 if k == 0 else me - 1}, device_id_type=MESH)

    @pl.when(me < tiles - 1)
    def _():
        pl.semaphore_signal(barrier, inc=1, device_id={"gx": me + 1}, device_id_type=MESH)

    @pl.when(me > 0)
    def _():
        pl.semaphore_signal(barrier, inc=1, device_id={"gx": me - 1}, device_id_type=MESH)

    inner = jnp.logical_and(me > 0, me < tiles - 1)

    @pl.when(inner)
    def _():
        pl.semaphore_wait(barrier, 2)

    @pl.when(jnp.logical_not(inner))
    def _():
        pl.semaphore_wait(barrier, 1)

    @pl.when(me < tiles - 1)
    def _():
        copy(0).start()

    @pl.when(me > 0)
    def _():
        copy(1).start()

    @pl.when(me < tiles - 1)
    def _():
        copy(0).wait_send()
        copy(1).wait_recv()

    @pl.when(me > 0)
    def _():
        copy(1).wait_send()
        copy(0).wait_recv()


def adjoint_kernel(
    tiles, u0, ub, q1, mine, near, mixing_t, coef, out,
    su0, sub, sq1, f1, f2, sout, parts, place_v, place_s, in_sem, place_sem, out_sem,
):
    me = lax.axis_index("gx")
    chans, rows, cols = u0.shape
    count = mine.shape[1]
    load_q = [pltpu.make_async_copy(q1.at[i], sq1.at[i], in_sem.at[i]) for i in range(rows + 2)]
    load_u = [pltpu.make_async_copy(u0.at[:, i, :], su0.at[i], in_sem.at[32 + i]) for i in range(rows)]
    load_b = [pltpu.make_async_copy(ub.at[:, i, :], sub.at[i], in_sem.at[64 + i]) for i in range(rows)]
    for group in range(3):
        block = mine[7:8, :] if group == 0 else near[group - 1, 7:8, :]
        place_v[group] = cell_rows(block, rows, cols)
    placing = pltpu.make_async_copy(place_v, place_s, place_sem)
    placing.start()
    for copy in load_q + load_u + load_b:
        copy.start()

    def clear(i, _):
        f2[i] = jnp.zeros((chans, cols), jnp.float32)
        return 0

    lax.fori_loop(0, rows + 6, clear, 0)

    def clear1(i, _):
        f1[i] = jnp.zeros((chans, cols), jnp.float32)
        return 0

    lax.fori_loop(0, rows + 4, clear1, 0)

    def contributions(block):
        full = jnp.concatenate([block, jnp.zeros((120, count), jnp.float32)], axis=0).T
        column = lambda k: full[:, k:k + 1]
        top, low = window_weights(column(7), [column(3 + k) for k in range(4)], rows, cols)
        for t in range(2):
            parts[2 * t] = column(t) * top
            parts[2 * t + 1] = column(t) * low

    def add(ref, line, chan, block, part, j):
        spot = (line, pl.ds(chan, 1), pl.ds(block, WIN))
        ref[spot] = ref[spot] + parts[part, pl.ds(j, 1), :]

    def place(group, j):
        return (
            place_s[group, 0, j], place_s[group, 1, j],
            pl.multiple_of(place_s[group, 2, j], 128))

    contributions(mine[...])
    placing.wait()

    def own(j4, _):
        for k in range(4):
            j = j4 * 4 + k
            line, chan, block = place(0, j)
            add(f1, line + 1, chan, block, 0, j)
            add(f2, line + 2, chan, block, 2, j)
            add(f1, line + 2, chan, block, 1, j)
            add(f2, line + 3, chan, block, 3, j)
        return 0

    lax.fori_loop(0, count // 4, own, 0)

    @pl.when(me > 0)
    def _():
        contributions(near[0])

        def lower(j, _):
            line, chan, block = place(1, j)

            @pl.when(line >= rows - 3)
            def _():
                spare1, spare2 = rows + 2, rows + 4
                at = line - (rows - 2)
                add(f2, jnp.where(at >= 0, at, spare2), chan, block, 2, j)
                add(f2, at + 1, chan, block, 3, j)
                at1 = line - (rows - 1)
                add(f1, jnp.where(at1 >= 0, at1, spare1), chan, block, 0, j)
                add(f1, jnp.where(at1 + 1 >= 0, at1 + 1, spare1), chan, block, 1, j)
            return 0

        lax.fori_loop(0, count, lower, 0)

    @pl.when(me < tiles - 1)
    def _():
        contributions(near[1])

        def upper(j, _):
            line, chan, block = place(2, j)

            @pl.when(line <= 1)
            def _():
                add(f2, line + rows + 2, chan, block, 2, j)
                add(f2, line + rows + 3, chan, block, 3, j)
                add(f1, line + rows + 1, chan, block, 0, j)
                add(f1, line + rows + 2, chan, block, 1, j)
            return 0

        lax.fori_loop(0, count, upper, 0)

    wide = widen_mix(mixing_t[...])
    coefs = coef_columns(coef, -1.0)
    for copy in load_q:
        copy.wait()

    def first(i, _):
        centre = f2[i + 1]
        out_rows = step_rows(centre, f2[i + 2], f2[i], coefs)
        f1[i] = f1[i] + out_rows + sq1[i] * mix_rows(wide, centre)
        return 0

    lax.fori_loop(0, rows + 2, first, 0)

    @pl.when(me == 0)
    def _():
        f1[0] = jnp.zeros((chans, cols), jnp.float32)

    @pl.when(me == tiles - 1)
    def _():
        f1[rows + 1] = jnp.zeros((chans, cols), jnp.float32)

    for copy in load_u + load_b:
        copy.wait()
    saves = [pltpu.make_async_copy(sout.at[i], out.at[:, i, :], out_sem.at[i]) for i in range(rows)]
    for i in range(rows):
        centre = f1[i + 1]
        state = su0[i]
        th = jnp.tanh(state)
        sout[i] = (
            (state - sub[i])
            + step_rows(centre, f1[i + 2], f1[i], coefs)
            + (1.0 - th * th) * mix_rows(wide, centre)
        )
        saves[i].start()
    for copy in saves:
        copy.wait()


def shards(
    initial, background, mixing, diffusion, advection, obs_values, obs_weight,
    interp_weights, stencil_index, station_tile, counts,
):
    num_fields, num_levels, rows, cols = initial.shape
    chans = num_fields * num_levels
    tiles = lax.axis_size("gx")
    held = obs_values.shape[1]
    most = max(2, held * 3 // (2 * tiles))
    cap = -(-most // 8) * 8
    slots = tiles * cap
    u0 = initial.reshape(chans, rows, cols)
    ub = background.reshape(chans, rows, cols)
    f32, i32 = jnp.float32, jnp.int32
    anyspace = pl.BlockSpec(memory_space=pl.ANY)
    vmem = pl.BlockSpec(memory_space=pltpu.VMEM)
    smem = pl.BlockSpec(memory_space=pltpu.SMEM)
    coef = jnp.concatenate(
        [diffusion.reshape(1, chans), advection.reshape(2, chans)], axis=0).T
    limit = 60 * 1024 * 1024
    recv, halo = pl.pallas_call(
        functools.partial(route_kernel, tiles, cap),
        out_shape=(
            jax.ShapeDtypeStruct((tiles, cap, 128), f32),
            jax.ShapeDtypeStruct((4, chans, cols), f32),
        ),
        in_specs=[vmem] * 5 + [smem, anyspace],
        out_specs=(vmem, anyspace),
        scratch_shapes=[
            pltpu.VMEM((tiles, cap, 128), f32),
            pltpu.SemaphoreType.DMA((tiles,)),
            pltpu.SemaphoreType.DMA((tiles,)),
            pltpu.SemaphoreType.DMA((4,)),
            pltpu.SemaphoreType.DMA((4,)),
        ],
        compiler_params=pltpu.CompilerParams(collective_id=0, has_side_effects=True),
    )(obs_values, obs_weight, interp_weights, stencil_index,
      station_tile.reshape(1, held), counts, u0)
    q1, packed = pl.pallas_call(
        functools.partial(forward_kernel, tiles),
        out_shape=(
            jax.ShapeDtypeStruct((rows + 2, chans, cols), f32),
            jax.ShapeDtypeStruct((8, slots), f32),
        ),
        in_specs=[anyspace, anyspace, vmem, vmem, vmem],
        out_specs=(anyspace, vmem),
        scratch_shapes=[
            pltpu.VMEM((rows + 4, chans, cols), f32),
            pltpu.VMEM((rows + 2, chans, cols), f32),
            pltpu.VMEM((rows, chans, cols), f32),
            pltpu.VMEM((rows + 2, chans, cols), f32),
            pltpu.VMEM((slots, WIN), f32),
            pltpu.VMEM((slots, WIN), f32),
            pltpu.VMEM((8, slots), i32),
            pltpu.SMEM((8, slots), i32),
            pltpu.SemaphoreType.DMA((rows + 4,)),
            pltpu.SemaphoreType.DMA((rows + 2,)),
            pltpu.SemaphoreType.DMA,
        ],
        compiler_params=pltpu.CompilerParams(vmem_limit_bytes=limit),
    )(u0, halo, recv, mixing, coef)
    near = pl.pallas_call(
        functools.partial(share_kernel, tiles),
        out_shape=jax.ShapeDtypeStruct((2, 8, slots), f32),
        in_specs=[vmem],
        out_specs=vmem,
        scratch_shapes=[pltpu.SemaphoreType.DMA((2,)), pltpu.SemaphoreType.DMA((2,))],
        compiler_params=pltpu.CompilerParams(collective_id=1, has_side_effects=True),
    )(packed)
    gradient = pl.pallas_call(
        functools.partial(adjoint_kernel, tiles),
        out_shape=jax.ShapeDtypeStruct((chans, rows, cols), f32),
        in_specs=[anyspace, anyspace, anyspace, vmem, vmem, vmem, vmem],
        out_specs=anyspace,
        scratch_shapes=[
            pltpu.VMEM((rows, chans, cols), f32),
            pltpu.VMEM((rows, chans, cols), f32),
            pltpu.VMEM((rows + 2, chans, cols), f32),
            pltpu.VMEM((rows + 4, chans, cols), f32),
            pltpu.VMEM((rows + 6, chans, cols), f32),
            pltpu.VMEM((rows, chans, cols), f32),
            pltpu.VMEM((4, slots, WIN), f32),
            pltpu.VMEM((3, 8, slots), i32),
            pltpu.SMEM((3, 8, slots), i32),
            pltpu.SemaphoreType.DMA((96,)),
            pltpu.SemaphoreType.DMA,
            pltpu.SemaphoreType.DMA((rows,)),
        ],
        compiler_params=pltpu.CompilerParams(vmem_limit_bytes=limit),
    )(u0, ub, q1, packed, near, mixing.T, coef)
    return gradient.reshape(num_fields, num_levels, rows, cols)


def solution(mesh):
    placed = (
        P("groups", None, "gx", None),
        P("groups", None, "gx", None),
        P(),
        P(),
        P(),
        P("groups", "gx"),
        P("groups", "gx"),
        P("groups", "gx"),
        P("groups", "gx"),
        P("gx", "groups"),
        P("groups", "gx"),
    )
    return jax.shard_map(
        shards, mesh=mesh, in_specs=placed, out_specs=P("groups", None, "gx", None), check_vma=False
    )
```

```python
import functools
import jax
import jax.numpy as jnp
from jax import lax
from jax.experimental import pallas as pl
from jax.experimental.pallas import tpu as pltpu
from jax.sharding import PartitionSpec as P

MESH = pl.DeviceIdType.MESH
WIN = 256


def fdot(a, b, dims):
    return lax.dot_general(a, b, (dims, ((), ())), preferred_element_type=jnp.float32)


def split3(v):
    hi = v.astype(jnp.bfloat16)
    rest = v - hi.astype(jnp.float32)
    mid = rest.astype(jnp.bfloat16)
    lo = (rest - mid.astype(jnp.float32)).astype(jnp.bfloat16)
    return hi, mid, lo


def widen_mix(m):
    hi = m.astype(jnp.bfloat16)
    lo = (m - hi.astype(jnp.float32)).astype(jnp.bfloat16)
    return jnp.concatenate([hi, hi, lo], axis=1)


def mix_rows(wide, v):
    hi = v.astype(jnp.bfloat16).astype(jnp.float32)
    parts = jnp.concatenate([hi, v - hi, hi], axis=0).astype(jnp.bfloat16)
    return fdot(wide, parts, ((1,), (0,)))


def shifts(v):
    cols = v.shape[1]
    lane = lax.broadcasted_iota(jnp.int32, v.shape, 1)
    east = jnp.where(lane == cols - 1, 0.0, pltpu.roll(v, cols - 1, 1))
    west = jnp.where(lane == 0, 0.0, pltpu.roll(v, 1, 1))
    return east, west


def step_rows(centre, above, below, coef):
    east, west = shifts(centre)
    return (
        coef[0] * centre + coef[1] * above + coef[2] * below + coef[3] * east + coef[4] * west
    )


def exact_dot(hot, v, dims):
    hi, mid, lo = split3(v)
    return fdot(hot, hi, dims) + fdot(hot, mid, dims) + fdot(hot, lo, dims)


def hot_of(condition):
    return condition.astype(jnp.float32).astype(jnp.bfloat16)


def coef_columns(coef_ref, sign):
    c, a, b = coef_ref[:, 0:1], sign * coef_ref[:, 1:2], sign * coef_ref[:, 2:3]
    return 1.0 - 4.0 * c, c + a, c - a, c + b, c - b


def channel_column(table, chans):
    fields, levels = table.shape
    row = lax.broadcasted_iota(jnp.int32, (chans, fields), 0)
    field = lax.broadcasted_iota(jnp.int32, (chans, fields), 1)
    total = None
    for level in range(levels):
        hot = hot_of(row == field * levels + level)
        part = exact_dot(hot, table, ((1,), (0,)))[:, level:level + 1]
        total = part if total is None else total + part
    return total


def window_weights(column, weights, cols):
    block = jnp.minimum(jnp.floor(column * (1.0 / 128)), float(cols // 128 - 2))
    local = column - 128.0 * block
    lane = lax.broadcasted_iota(jnp.int32, (column.shape[0], WIN), 1).astype(jnp.float32)
    left, right = lane == local, lane == local + 1.0
    top = jnp.where(left, weights[0], 0.0) + jnp.where(right, weights[1], 0.0)
    low = jnp.where(left, weights[2], 0.0) + jnp.where(right, weights[3], 0.0)
    return top, low


def split_cell(cell, rows, cols):
    chan = jnp.floor(cell * (1.0 / (rows * cols)))
    rest = cell - chan * (rows * cols)
    line = jnp.floor(rest * (1.0 / cols))
    return line, chan, rest - line * cols


def place_rows(line, chan, column, count, cols):
    block = jnp.minimum(jnp.floor(column * (1.0 / 128)), float(cols // 128 - 2)) * 128.0
    zero = jnp.zeros_like(line)
    return jnp.concatenate([line, chan, block, count] + [zero] * 4, axis=0).astype(jnp.int32)


def forward_kernel(
    tiles, cap, vals, wts, interp, cells, target, count, diffusion, advection, mixing, u0,
    q1, mine, near, coef_out, mixing_t,
    send, recv, su0, su1, su2, sq1, hots, outbox,
    in_sem, out_sem, send_sem, recv_sem, halo_send, halo_recv, near_send, near_recv,
):
    me = lax.axis_index("gx")
    chans, rows, cols = u0.shape
    held = target.shape[1]
    slots = tiles * cap
    nt = ((1,), (1,))
    loads = [
        pltpu.make_async_copy(u0.at[:, r, :], su0.at[r + 2], in_sem.at[r]) for r in range(rows)
    ]
    for copy in loads:
        copy.start()
    barrier = pltpu.get_barrier_semaphore()

    def greet(d, _):
        pl.semaphore_signal(
            barrier, inc=1, device_id={"gx": lax.rem(me + d, tiles)}, device_id_type=MESH
        )
        return 0

    lax.fori_loop(1, tiles, greet, 0)
    names = target[...]
    match = (lax.broadcasted_iota(jnp.int32, (tiles, held), 0) == names).astype(jnp.float32)
    before = hot_of(
        lax.broadcasted_iota(jnp.int32, (held, held), 0)
        < lax.broadcasted_iota(jnp.int32, (held, held), 1)
    )
    ranks = fdot(match.astype(jnp.bfloat16), before, ((1,), (0,)))
    rank = jnp.sum(match * ranks, axis=0, keepdims=True).astype(jnp.int32)
    position = names * cap + rank
    hot = hot_of(lax.broadcasted_iota(jnp.int32, (slots, held), 0) == position)
    live = lax.broadcasted_iota(jnp.int32, (1, held), 1) < count[0, 0]
    weight = jnp.where(live, wts[...], 0.0)
    recs = jnp.concatenate(
        [vals[...], weight, interp[...], cells[0:1, :].astype(jnp.float32),
         jnp.zeros((120, held), jnp.float32)], axis=0)
    send[...] = exact_dot(hot, recs, nt).reshape(tiles, cap, 128)
    pl.semaphore_wait(barrier, tiles - 1)

    def edge(up, k):
        if up:
            src, dst, at, to = rows - 2 + k, k, k, me + 1
        else:
            src, dst, at, to = k, rows + 2 + k, 2 + k, me - 1
        return pltpu.make_async_remote_copy(
            src_ref=u0.at[:, src, :], dst_ref=su0.at[dst],
            send_sem=halo_send.at[at], recv_sem=halo_recv.at[at],
            device_id={"gx": to}, device_id_type=MESH)

    def parcel(d, to, row):
        return pltpu.make_async_remote_copy(
            src_ref=send.at[to], dst_ref=recv.at[row],
            send_sem=send_sem.at[d], recv_sem=recv_sem.at[d],
            device_id={"gx": to}, device_id_type=MESH)

    def start(d, _):
        parcel(d, lax.rem(me + d, tiles), me).start()
        return 0

    def finish(d, _):
        parcel(d, lax.rem(me + d, tiles), me).wait_send()
        source = lax.rem(me + tiles - d, tiles)
        parcel(d, source, source).wait_recv()
        return 0

    lax.fori_loop(1, tiles, start, 0)

    @pl.when(me < tiles - 1)
    def _():
        edge(True, 1).start()
        edge(True, 0).start()

    @pl.when(me > 0)
    def _():
        edge(False, 0).start()
        edge(False, 1).start()

    recv[me] = send[me]
    columns = [channel_column(t, chans) for t in (diffusion[...], advection[0], advection[1])]
    lane = lax.broadcasted_iota(jnp.int32, (chans, 128), 1)
    coef_out[...] = jnp.where(
        lane == 0, columns[0], jnp.where(lane == 1, columns[1], columns[2]))
    mixing_t[...] = mixing[...].T
    wide = widen_mix(mixing[...])
    coefs = coef_columns(coef_out, 1.0)

    def first(i, _):
        centre = su0[i + 1]
        su1[i] = step_rows(centre, su0[i + 2], su0[i], coefs) + mix_rows(wide, jnp.tanh(centre))
        return 0

    for copy in loads:
        copy.wait()
    lax.fori_loop(2, rows, first, 0)

    lax.fori_loop(1, tiles, finish, 0)
    records = recv[...].reshape(slots, 128)
    turned = records.T
    weights = turned[2:3, :]
    line, chan, column = split_cell(turned[7:8, :], rows, cols)
    ahead = hot_of(
        lax.broadcasted_iota(jnp.int32, (slots, slots), 0)
        < lax.broadcasted_iota(jnp.int32, (slots, slots), 1)
    )
    alive = (weights > 0.0).astype(jnp.float32)
    masks = jnp.concatenate(
        [alive, jnp.where(line >= rows - 3, alive, 0.0), jnp.where(line <= 1.0, alive, 0.0),
         jnp.zeros((5, slots), jnp.float32)], axis=0)
    order = fdot(masks.astype(jnp.bfloat16), ahead, ((1,), (0,)))
    spot = jnp.where(masks > 0.0, order, -1.0).astype(jnp.int32)
    totals = jnp.sum(masks, axis=1, keepdims=True)
    slot = lax.broadcasted_iota(jnp.int32, (slots, slots), 0)
    for k in range(3):
        hots[k] = hot_of(slot == spot[k:k + 1, :])

    @pl.when(me < tiles - 1)
    def _():
        for k in range(2):
            edge(True, k).wait_send()
            edge(False, k).wait_recv()

    @pl.when(me > 0)
    def _():
        for k in range(2):
            edge(False, k).wait_send()
            edge(True, k).wait_recv()

    blank = jnp.zeros((chans, cols), jnp.float32)

    @pl.when(me == 0)
    def _():
        su0[0] = blank
        su0[1] = blank

    @pl.when(me == tiles - 1)
    def _():
        su0[rows + 2] = blank
        su0[rows + 3] = blank

    def outer(k, _):
        return first(jnp.where(k < 2, k, rows - 2 + k), 0)

    lax.fori_loop(0, 4, outer, 0)

    @pl.when(me == 0)
    def _():
        su1[0] = blank

    @pl.when(me == tiles - 1)
    def _():
        su1[rows + 1] = blank

    stores = lambda i: pltpu.make_async_copy(sq1.at[i], q1.at[i], out_sem.at[i])

    def second(i, _):
        centre = su1[i + 1]
        th = jnp.tanh(centre)
        sq1[i + 1] = 1.0 - th * th
        stores(i + 1).start()
        su2[i] = step_rows(centre, su1[i + 2], su1[i], coefs) + mix_rows(wide, th)
        return 0

    for i in (0, rows + 1):
        th = jnp.tanh(su1[i])
        sq1[i] = 1.0 - th * th
        stores(i).start()
    lax.fori_loop(0, rows, second, 0)
    col = lambda k: records[:, k:k + 1]
    line_c, chan_c, column_c = split_cell(col(7), rows, cols)
    span = (rows - 1) * chans
    flat = lax.broadcasted_iota(jnp.int32, (slots, span), 1).astype(jnp.float32)
    pick = hot_of(flat == line_c * chans + chan_c)
    results = []

    def picked(state, first_row, start):
        block = state[first_row:first_row + rows - 1, :, start:start + WIN].reshape(span, WIN)
        hi = block.astype(jnp.bfloat16)
        rest = (block - hi.astype(jnp.float32)).astype(jnp.bfloat16)
        return fdot(pick, hi, ((1,), (0,))) + fdot(pick, rest, ((1,), (0,)))

    for which, (state, base) in enumerate(((su1, 1), (su2, 0))):
        sample = jnp.zeros((slots, WIN), jnp.float32)
        for start in range(0, cols, WIN):
            lane = lax.broadcasted_iota(jnp.int32, (slots, WIN), 1).astype(jnp.float32)
            local = column_c - float(start)
            left, right = lane == local, lane == local + 1.0
            top = jnp.where(left, col(3), 0.0) + jnp.where(right, col(4), 0.0)
            low = jnp.where(left, col(5), 0.0) + jnp.where(right, col(6), 0.0)
            sample += picked(state, base, start) * top + picked(state, base + 1, start) * low
        sample = jnp.sum(sample, axis=1, keepdims=True)
        results.append(col(2) * (sample - col(which)))
    lane = lax.broadcasted_iota(jnp.int32, records.shape, 1)
    merged = jnp.where(lane == 0, results[0], jnp.where(lane == 1, results[1], 0.0)).T
    zero = jnp.zeros((7, slots), jnp.float32)
    for k, moved in ((1, -rows), (2, rows), (0, 0)):
        fields = jnp.concatenate(
            [merged[0:2, :], line + float(moved), turned[3:7, :], chan, column, zero], axis=0)
        hi, mid, lo = split3(fields)
        packed = fdot(hi, hots[k], nt) + fdot(mid, hots[k], nt) + fdot(lo, hots[k], nt)
        field = lax.broadcasted_iota(jnp.int32, packed.shape, 0)
        packed = jnp.where(field == 9, totals[k:k + 1, :], packed)
        if k == 0:
            mine[...] = packed
        else:
            outbox[k - 1] = packed

    def note(k):
        return pltpu.make_async_remote_copy(
            src_ref=outbox.at[k], dst_ref=near.at[k],
            send_sem=near_send.at[k], recv_sem=near_recv.at[k],
            device_id={"gx": me + 1 if k == 0 else me - 1}, device_id_type=MESH)

    @pl.when(me < tiles - 1)
    def _():
        note(0).start()

    @pl.when(me > 0)
    def _():
        note(1).start()

    for i in range(rows + 2):
        stores(i).wait()

    @pl.when(me == 0)
    def _():
        near[0] = jnp.zeros((16, slots), jnp.float32)

    @pl.when(me == tiles - 1)
    def _():
        near[1] = jnp.zeros((16, slots), jnp.float32)

    @pl.when(me < tiles - 1)
    def _():
        note(0).wait_send()
        note(1).wait_recv()

    @pl.when(me > 0)
    def _():
        note(1).wait_send()
        note(0).wait_recv()


def adjoint_kernel(
    tiles, u0, ub, q1, mine, near, mixing_t, coef, out,
    su0, sub, sq1, f1, f2, sout, parts, place_v, place_s, in_sem, place_sem, out_sem,
):
    me = lax.axis_index("gx")
    chans, rows, cols = u0.shape
    slots = mine.shape[1]
    load_q = [pltpu.make_async_copy(q1.at[i], sq1.at[i], in_sem.at[0, i]) for i in range(rows + 2)]
    load_u = [pltpu.make_async_copy(u0.at[:, i, :], su0.at[i], in_sem.at[1, i]) for i in range(rows)]
    load_b = [pltpu.make_async_copy(ub.at[:, i, :], sub.at[i], in_sem.at[2, i]) for i in range(rows)]
    lists = [mine[...], near[0], near[1]]
    for group, block in enumerate(lists):
        place_v[group] = place_rows(
            block[2:3, :] + 3.0, block[7:8, :], block[8:9, :], block[9:10, :], cols)
    placing = pltpu.make_async_copy(place_v, place_s, place_sem)
    placing.start()
    for copy in load_q + load_u + load_b:
        copy.start()

    def clear(i, _):
        f1[i] = jnp.zeros((chans, cols), jnp.float32)
        f2[i] = jnp.zeros((chans, cols), jnp.float32)
        return 0

    lax.fori_loop(0, rows + 6, clear, 0)
    placing.wait()
    for group in range(3):
        amount = place_s[group, 3, 0]
        for start in range(0, slots, 128):

            @pl.when(amount > start)
            def _():
                block = (mine if group == 0 else near.at[group - 1])[:, start:start + 128]
                full = jnp.concatenate([block, jnp.zeros((112, 128), jnp.float32)], axis=0).T
                col = lambda k: full[:, k:k + 1]
                top, low = window_weights(col(8), [col(3 + k) for k in range(4)], cols)
                parts[0] = col(0) * top
                parts[1] = col(0) * low
                parts[2] = col(1) * top
                parts[3] = col(1) * low

                def add(j2, _):
                    for k in range(2):
                        j = j2 * 2 + k
                        at, ch = place_s[group, 0, start + j], place_s[group, 1, start + j]
                        block = pl.multiple_of(place_s[group, 2, start + j], 128)
                        spots = [
                            (ref, (at + step, pl.ds(ch, 1), pl.ds(block, WIN)), 2 * t + step)
                            for t, ref in enumerate((f1, f2)) for step in range(2)]
                        sums = [
                            ref[spot] + parts[part, pl.ds(j, 1), :] for ref, spot, part in spots]
                        for (ref, spot, _), total in zip(spots, sums):
                            ref[spot] = total
                    return 0

                lax.fori_loop(0, (jnp.minimum(amount - start, 128) + 1) // 2, add, 0)

    wide = widen_mix(mixing_t[...])
    coefs = coef_columns(coef, -1.0)
    for copy in load_q:
        copy.wait()

    def first(i, _):
        centre = f2[i + 2]
        spread = step_rows(centre, f2[i + 3], f2[i + 1], coefs)
        f1[i + 2] = f1[i + 2] + spread + sq1[i] * mix_rows(wide, centre)
        return 0

    lax.fori_loop(0, rows + 2, first, 0)

    @pl.when(me == 0)
    def _():
        f1[2] = jnp.zeros((chans, cols), jnp.float32)

    @pl.when(me == tiles - 1)
    def _():
        f1[rows + 3] = jnp.zeros((chans, cols), jnp.float32)

    for copy in load_u + load_b:
        copy.wait()
    save = lambda i: pltpu.make_async_copy(sout.at[i], out.at[:, i, :], out_sem.at[i])
    for i in range(rows):
        centre = f1[i + 3]
        state = su0[i]
        th = jnp.tanh(state)
        sout[i] = (
            (state - sub[i])
            + step_rows(centre, f1[i + 4], f1[i + 2], coefs)
            + (1.0 - th * th) * mix_rows(wide, centre)
        )
        save(i).start()
    for i in range(rows):
        save(i).wait()


def shards(
    initial, background, mixing, diffusion, advection, obs_values, obs_weight,
    interp_weights, stencil_index, station_tile, counts,
):
    num_fields, num_levels, rows, cols = initial.shape
    chans = num_fields * num_levels
    tiles = lax.axis_size("gx")
    held = obs_values.shape[1]
    most = max(2, held * 3 // (2 * tiles))
    cap = -(-most // 8) * 8
    slots = tiles * cap
    u0 = initial.reshape(chans, rows, cols)
    ub = background.reshape(chans, rows, cols)
    f32, i32 = jnp.float32, jnp.int32
    anyspace = pl.BlockSpec(memory_space=pl.ANY)
    vmem = pl.BlockSpec(memory_space=pltpu.VMEM)
    smem = pl.BlockSpec(memory_space=pltpu.SMEM)
    dma = pltpu.SemaphoreType.DMA
    limit = 60 * 1024 * 1024
    shape = jax.ShapeDtypeStruct
    q1, mine, near, coef, mixing_t = pl.pallas_call(
        functools.partial(forward_kernel, tiles, cap),
        out_shape=(
            shape((rows + 2, chans, cols), f32),
            shape((16, slots), f32),
            shape((2, 16, slots), f32),
            shape((chans, 128), f32),
            shape((chans, chans), f32),
        ),
        in_specs=[vmem] * 5 + [smem] + [vmem] * 3 + [anyspace],
        out_specs=(anyspace, vmem, vmem, vmem, vmem),
        scratch_shapes=[
            pltpu.VMEM((tiles, cap, 128), f32),
            pltpu.VMEM((tiles, cap, 128), f32),
            pltpu.VMEM((rows + 4, chans, cols), f32),
            pltpu.VMEM((rows + 2, chans, cols), f32),
            pltpu.VMEM((rows, chans, cols), f32),
            pltpu.VMEM((rows + 2, chans, cols), f32),
            pltpu.VMEM((3, slots, slots), jnp.bfloat16),
            pltpu.VMEM((2, 16, slots), f32),
            dma((rows,)),
            dma((rows + 2,)),
            dma((tiles,)),
            dma((tiles,)),
            dma((4,)),
            dma((4,)),
            dma((2,)),
            dma((2,)),
        ],
        compiler_params=pltpu.CompilerParams(
            collective_id=0, has_side_effects=True, vmem_limit_bytes=limit),
    )(obs_values, obs_weight, interp_weights, stencil_index,
      station_tile.reshape(1, held), counts, diffusion, advection, mixing, u0)
    gradient = pl.pallas_call(
        functools.partial(adjoint_kernel, tiles),
        out_shape=shape((chans, rows, cols), f32),
        in_specs=[anyspace, anyspace, anyspace, vmem, vmem, vmem, vmem],
        out_specs=anyspace,
        scratch_shapes=[
            pltpu.VMEM((rows, chans, cols), f32),
            pltpu.VMEM((rows, chans, cols), f32),
            pltpu.VMEM((rows + 2, chans, cols), f32),
            pltpu.VMEM((rows + 6, chans, cols), f32),
            pltpu.VMEM((rows + 6, chans, cols), f32),
            pltpu.VMEM((rows, chans, cols), f32),
            pltpu.VMEM((4, 128, WIN), f32),
            pltpu.VMEM((3, 8, slots), i32),
            pltpu.SMEM((3, 8, slots), i32),
            dma((3, rows + 2)),
            dma,
            dma((rows,)),
        ],
        compiler_params=pltpu.CompilerParams(vmem_limit_bytes=limit),
    )(u0, ub, q1, mine, near, mixing_t, coef)
    return gradient.reshape(num_fields, num_levels, rows, cols)


def solution(mesh):
    placed = (
        P("groups", None, "gx", None),
        P("groups", None, "gx", None),
        P(),
        P(),
        P(),
        P("groups", "gx"),
        P("groups", "gx"),
        P("groups", "gx"),
        P("groups", "gx"),
        P("gx", "groups"),
        P("groups", "gx"),
    )
    return jax.shard_map(
        shards, mesh=mesh, in_specs=placed, out_specs=P("groups", None, "gx", None), check_vma=False
    )
```

```python
import functools
import jax
import jax.numpy as jnp
from jax import lax
from jax.experimental import pallas as pl
from jax.experimental.pallas import tpu as pltpu
from jax.sharding import PartitionSpec as P

MESH = pl.DeviceIdType.MESH
WIN = 256


def fdot(a, b, dims):
    return lax.dot_general(a, b, (dims, ((), ())), preferred_element_type=jnp.float32)


def split3(v):
    hi = v.astype(jnp.bfloat16)
    rest = v - hi.astype(jnp.float32)
    mid = rest.astype(jnp.bfloat16)
    lo = (rest - mid.astype(jnp.float32)).astype(jnp.bfloat16)
    return hi, mid, lo


def widen_mix(m):
    hi = m.astype(jnp.bfloat16)
    lo = (m - hi.astype(jnp.float32)).astype(jnp.bfloat16)
    return jnp.concatenate([hi, hi, lo], axis=1)


def mix_rows(wide, v):
    hi = v.astype(jnp.bfloat16).astype(jnp.float32)
    parts = jnp.concatenate([hi, v - hi, hi], axis=0).astype(jnp.bfloat16)
    return fdot(wide, parts, ((1,), (0,)))


def shifts(v):
    cols = v.shape[1]
    lane = lax.broadcasted_iota(jnp.int32, (v.shape[0], 128), 1)
    east, west = pltpu.roll(v, cols - 1, 1), pltpu.roll(v, 1, 1)
    last = jnp.where(lane == 127, 0.0, east[:, cols - 128:])
    start = jnp.where(lane == 0, 0.0, west[:, :128])
    east = jnp.concatenate([east[:, :cols - 128], last], axis=1)
    west = jnp.concatenate([start, west[:, 128:]], axis=1)
    return east, west


def step_rows(centre, above, below, coef):
    east, west = shifts(centre)
    return (
        coef[0] * centre + coef[1] * above + coef[2] * below + coef[3] * east + coef[4] * west
    )


def exact_dot(hot, v, dims):
    hi, mid, lo = split3(v)
    return fdot(hot, hi, dims) + fdot(hot, mid, dims) + fdot(hot, lo, dims)


def hot_of(condition):
    return condition.astype(jnp.float32).astype(jnp.bfloat16)


def coef_columns(coef_ref, sign):
    c, a, b = coef_ref[:, 0:1], sign * coef_ref[:, 1:2], sign * coef_ref[:, 2:3]
    return 1.0 - 4.0 * c, c + a, c - a, c + b, c - b


def channel_column(table, chans):
    levels, fields = table.shape
    row = lax.broadcasted_iota(jnp.int32, (chans, fields), 0)
    field = lax.broadcasted_iota(jnp.int32, (chans, fields), 1)
    total = None
    for level in range(levels):
        hot = hot_of(row == field * levels + level)
        part = exact_dot(hot, table, ((1,), (1,)))[:, level:level + 1]
        total = part if total is None else total + part
    return total


def window_weights(column, weights, cols):
    block = jnp.minimum(jnp.floor(column * (1.0 / 128)), float(cols // 128 - 2))
    local = column - 128.0 * block
    lane = lax.broadcasted_iota(jnp.int32, (column.shape[0], WIN), 1).astype(jnp.float32)
    left, right = lane == local, lane == local + 1.0
    top = jnp.where(left, weights[0], 0.0) + jnp.where(right, weights[1], 0.0)
    low = jnp.where(left, weights[2], 0.0) + jnp.where(right, weights[3], 0.0)
    return top, low


def split_cell(cell, rows, cols):
    chan = jnp.floor(cell * (1.0 / (rows * cols)))
    rest = cell - chan * (rows * cols)
    line = jnp.floor(rest * (1.0 / cols))
    return line, chan, rest - line * cols


def place_rows(line, chan, column, count, cols):
    block = jnp.minimum(jnp.floor(column * (1.0 / 128)), float(cols // 128 - 2)) * 128.0
    zero = jnp.zeros_like(line)
    return jnp.concatenate([line, chan, block, count] + [zero] * 4, axis=0).astype(jnp.int32)


def forward_kernel(
    tiles, cap, vals, wts, interp, cells, target, count, diffusion, advection, mixing, u0,
    q1, mine, near, coef_out, mixing_t,
    send, recv, su0, su1, su2, sq1, hots, outbox,
    in_sem, out_sem, send_sem, recv_sem, halo_send, halo_recv, near_send, near_recv,
):
    me = lax.axis_index("gx")
    chans, rows, cols = u0.shape
    held = target.shape[1]
    slots = tiles * cap
    nt = ((1,), (1,))
    loads = [
        pltpu.make_async_copy(u0.at[:, r, :], su0.at[r + 2], in_sem.at[r]) for r in range(rows)
    ]
    for copy in loads:
        copy.start()
    barrier = pltpu.get_barrier_semaphore()

    def greet(d, _):
        pl.semaphore_signal(
            barrier, inc=1, device_id={"gx": lax.rem(me + d, tiles)}, device_id_type=MESH
        )
        return 0

    lax.fori_loop(1, tiles, greet, 0)
    names = target[...]
    match = (lax.broadcasted_iota(jnp.int32, (tiles, held), 0) == names).astype(jnp.float32)
    before = hot_of(
        lax.broadcasted_iota(jnp.int32, (held, held), 0)
        < lax.broadcasted_iota(jnp.int32, (held, held), 1)
    )
    ranks = fdot(match.astype(jnp.bfloat16), before, ((1,), (0,)))
    rank = jnp.sum(match * ranks, axis=0, keepdims=True).astype(jnp.int32)
    position = names * cap + rank
    hot = hot_of(lax.broadcasted_iota(jnp.int32, (slots, held), 0) == position)
    live = lax.broadcasted_iota(jnp.int32, (1, held), 1) < count[0, 0]
    weight = jnp.where(live, wts[...], 0.0)
    recs = jnp.concatenate(
        [vals[...], weight, interp[...], cells[0:1, :].astype(jnp.float32),
         jnp.zeros((120, held), jnp.float32)], axis=0)
    send[...] = exact_dot(hot, recs, nt).reshape(tiles, cap, 128)
    pl.semaphore_wait(barrier, tiles - 1)

    def edge(up, k):
        if up:
            src, dst, at, to = rows - 2 + k, k, k, me + 1
        else:
            src, dst, at, to = k, rows + 2 + k, 2 + k, me - 1
        return pltpu.make_async_remote_copy(
            src_ref=u0.at[:, src, :], dst_ref=su0.at[dst],
            send_sem=halo_send.at[at], recv_sem=halo_recv.at[at],
            device_id={"gx": to}, device_id_type=MESH)

    def parcel(d, to, row):
        return pltpu.make_async_remote_copy(
            src_ref=send.at[to], dst_ref=recv.at[row],
            send_sem=send_sem.at[d], recv_sem=recv_sem.at[d],
            device_id={"gx": to}, device_id_type=MESH)

    def start(d, _):
        parcel(d, lax.rem(me + d, tiles), me).start()
        return 0

    def finish(d, _):
        parcel(d, lax.rem(me + d, tiles), me).wait_send()
        source = lax.rem(me + tiles - d, tiles)
        parcel(d, source, source).wait_recv()
        return 0

    lax.fori_loop(1, tiles, start, 0)

    @pl.when(me < tiles - 1)
    def _():
        edge(True, 1).start()
        edge(True, 0).start()

    @pl.when(me > 0)
    def _():
        edge(False, 0).start()
        edge(False, 1).start()

    recv[me] = send[me]
    columns = [channel_column(t, chans) for t in (diffusion[...], advection[0], advection[1])]
    lane = lax.broadcasted_iota(jnp.int32, (chans, 128), 1)
    coef_out[...] = jnp.where(
        lane == 0, columns[0], jnp.where(lane == 1, columns[1], columns[2]))
    mixing_t[...] = mixing[...].T
    wide = widen_mix(mixing[...])
    coefs = coef_columns(coef_out, 1.0)

    def first(i, _):
        centre = su0[i + 1]
        su1[i] = step_rows(centre, su0[i + 2], su0[i], coefs) + mix_rows(wide, jnp.tanh(centre))
        return 0

    for copy in loads:
        copy.wait()
    lax.fori_loop(2, rows, first, 0)

    lax.fori_loop(1, tiles, finish, 0)
    records = recv[...].reshape(slots, 128)
    turned = records.T
    weights = turned[2:3, :]
    line, chan, column = split_cell(turned[7:8, :], rows, cols)
    ahead = hot_of(
        lax.broadcasted_iota(jnp.int32, (slots, slots), 0)
        < lax.broadcasted_iota(jnp.int32, (slots, slots), 1)
    )
    alive = (weights > 0.0).astype(jnp.float32)
    masks = jnp.concatenate(
        [alive, jnp.where(line >= rows - 3, alive, 0.0), jnp.where(line <= 1.0, alive, 0.0),
         jnp.zeros((5, slots), jnp.float32)], axis=0)
    order = fdot(masks.astype(jnp.bfloat16), ahead, ((1,), (0,)))
    spot = jnp.where(masks > 0.0, order, -1.0).astype(jnp.int32)
    totals = jnp.sum(masks, axis=1, keepdims=True)
    slot = lax.broadcasted_iota(jnp.int32, (slots, slots), 0)
    for k in range(3):
        hots[k] = hot_of(slot == spot[k:k + 1, :])

    @pl.when(me < tiles - 1)
    def _():
        for k in range(2):
            edge(True, k).wait_send()
            edge(False, k).wait_recv()

    @pl.when(me > 0)
    def _():
        for k in range(2):
            edge(False, k).wait_send()
            edge(True, k).wait_recv()

    blank = jnp.zeros((chans, cols), jnp.float32)

    @pl.when(me == 0)
    def _():
        su0[0] = blank
        su0[1] = blank

    @pl.when(me == tiles - 1)
    def _():
        su0[rows + 2] = blank
        su0[rows + 3] = blank

    def outer(k, _):
        return first(jnp.where(k < 2, k, rows - 2 + k), 0)

    lax.fori_loop(0, 4, outer, 0)

    @pl.when(me == 0)
    def _():
        su1[0] = blank

    @pl.when(me == tiles - 1)
    def _():
        su1[rows + 1] = blank

    stores = lambda i: pltpu.make_async_copy(sq1.at[i], q1.at[i], out_sem.at[i])

    def second(i, _):
        centre = su1[i + 1]
        th = jnp.tanh(centre)
        sq1[i + 1] = 1.0 - th * th
        stores(i + 1).start()
        su2[i] = step_rows(centre, su1[i + 2], su1[i], coefs) + mix_rows(wide, th)
        return 0

    for i in (0, rows + 1):
        th = jnp.tanh(su1[i])
        sq1[i] = 1.0 - th * th
        stores(i).start()
    lax.fori_loop(0, rows, second, 0)
    col = lambda k: records[:, k:k + 1]
    line_c, chan_c, column_c = split_cell(col(7), rows, cols)
    span = (rows - 1) * chans
    flat = lax.broadcasted_iota(jnp.int32, (slots, span), 1).astype(jnp.float32)
    pick = hot_of(flat == line_c * chans + chan_c)
    pick = jnp.concatenate([pick, pick], axis=1)

    def picked(state, first_row, start):
        block = state[first_row:first_row + rows - 1, :, start:start + WIN].reshape(span, WIN)
        hi = block.astype(jnp.bfloat16).astype(jnp.float32)
        both = jnp.concatenate([hi, block - hi], axis=0).astype(jnp.bfloat16)
        return fdot(pick, both, ((1,), (0,)))

    samples = [jnp.zeros((slots, 1), jnp.float32)] * 2
    lane = lax.broadcasted_iota(jnp.int32, (slots, WIN), 1).astype(jnp.float32)
    for start in range(0, cols, WIN):
        local = column_c - float(start)
        left, right = lane == local, lane == local + 1.0
        top = jnp.where(left, col(3), jnp.where(right, col(4), 0.0))
        low = jnp.where(left, col(5), jnp.where(right, col(6), 0.0))
        for which, (state, base) in enumerate(((su1, 1), (su2, 0))):
            found = picked(state, base, start) * top + picked(state, base + 1, start) * low
            samples[which] = samples[which] + jnp.sum(found, axis=1, keepdims=True)
    results = [col(2) * (samples[k] - col(k)) for k in range(2)]
    lane = lax.broadcasted_iota(jnp.int32, records.shape, 1)
    merged = jnp.where(lane == 0, results[0], jnp.where(lane == 1, results[1], 0.0)).T
    zero = jnp.zeros((7, slots), jnp.float32)
    for k, moved in ((1, -rows), (2, rows), (0, 0)):
        fields = jnp.concatenate(
            [merged[0:2, :], line + float(moved), turned[3:7, :], chan, column, zero], axis=0)
        hi, mid, lo = split3(fields)
        packed = fdot(hi, hots[k], nt) + fdot(mid, hots[k], nt) + fdot(lo, hots[k], nt)
        field = lax.broadcasted_iota(jnp.int32, packed.shape, 0)
        packed = jnp.where(field == 9, totals[k:k + 1, :], packed)
        if k == 0:
            mine[...] = packed
        else:
            outbox[k - 1] = packed

    def note(k):
        return pltpu.make_async_remote_copy(
            src_ref=outbox.at[k], dst_ref=near.at[k],
            send_sem=near_send.at[k], recv_sem=near_recv.at[k],
            device_id={"gx": me + 1 if k == 0 else me - 1}, device_id_type=MESH)

    @pl.when(me < tiles - 1)
    def _():
        note(0).start()

    @pl.when(me > 0)
    def _():
        note(1).start()

    for i in range(rows + 2):
        stores(i).wait()

    @pl.when(me == 0)
    def _():
        near[0] = jnp.zeros((16, slots), jnp.float32)

    @pl.when(me == tiles - 1)
    def _():
        near[1] = jnp.zeros((16, slots), jnp.float32)

    @pl.when(me < tiles - 1)
    def _():
        note(0).wait_send()
        note(1).wait_recv()

    @pl.when(me > 0)
    def _():
        note(1).wait_send()
        note(0).wait_recv()


def adjoint_kernel(
    tiles, u0, ub, q1, mine, near, mixing_t, coef, out,
    su0, sub, sq1, f1, f2, sout, parts, place_v, place_s, in_sem, place_sem, out_sem,
):
    me = lax.axis_index("gx")
    chans, rows, cols = u0.shape
    slots = mine.shape[1]
    load_q = [pltpu.make_async_copy(q1.at[i], sq1.at[i], in_sem.at[0, i]) for i in range(rows + 2)]
    load_u = [pltpu.make_async_copy(u0.at[:, i, :], su0.at[i], in_sem.at[1, i]) for i in range(rows)]
    load_b = [pltpu.make_async_copy(ub.at[:, i, :], sub.at[i], in_sem.at[2, i]) for i in range(rows)]
    lists = [mine[...], near[0], near[1]]
    for group, block in enumerate(lists):
        place_v[group] = place_rows(
            block[2:3, :] + 3.0, block[7:8, :], block[8:9, :], block[9:10, :], cols)
    placing = pltpu.make_async_copy(place_v, place_s, place_sem)
    placing.start()
    for copy in load_q + load_u + load_b:
        copy.start()

    def clear(i, _):
        f1[i] = jnp.zeros((chans, cols), jnp.float32)
        f2[i] = jnp.zeros((chans, cols), jnp.float32)
        return 0

    lax.fori_loop(0, rows + 6, clear, 0)
    placing.wait()
    for group in range(3):
        amount = place_s[group, 3, 0]
        for start in range(0, slots, 128):

            @pl.when(amount > start)
            def _():
                block = (mine if group == 0 else near.at[group - 1])[:, start:start + 128]
                full = jnp.concatenate([block, jnp.zeros((112, 128), jnp.float32)], axis=0).T
                col = lambda k: full[:, k:k + 1]
                top, low = window_weights(col(8), [col(3 + k) for k in range(4)], cols)
                parts[0] = col(0) * top
                parts[1] = col(0) * low
                parts[2] = col(1) * top
                parts[3] = col(1) * low

                def add(j2, _):
                    for k in range(2):
                        j = j2 * 2 + k
                        at, ch = place_s[group, 0, start + j], place_s[group, 1, start + j]
                        block = pl.multiple_of(place_s[group, 2, start + j], 128)
                        spots = [
                            (ref, (at + step, pl.ds(ch, 1), pl.ds(block, WIN)), 2 * t + step)
                            for t, ref in enumerate((f1, f2)) for step in range(2)]
                        sums = [
                            ref[spot] + parts[part, pl.ds(j, 1), :] for ref, spot, part in spots]
                        for (ref, spot, _), total in zip(spots, sums):
                            ref[spot] = total
                    return 0

                lax.fori_loop(0, (jnp.minimum(amount - start, 128) + 1) // 2, add, 0)

    wide = widen_mix(mixing_t[...])
    coefs = coef_columns(coef, -1.0)
    for copy in load_q:
        copy.wait()

    def first(i, _):
        centre = f2[i + 2]
        spread = step_rows(centre, f2[i + 3], f2[i + 1], coefs)
        f1[i + 2] = f1[i + 2] + spread + sq1[i] * mix_rows(wide, centre)
        return 0

    lax.fori_loop(0, rows + 2, first, 0)

    @pl.when(me == 0)
    def _():
        f1[2] = jnp.zeros((chans, cols), jnp.float32)

    @pl.when(me == tiles - 1)
    def _():
        f1[rows + 3] = jnp.zeros((chans, cols), jnp.float32)

    for copy in load_u + load_b:
        copy.wait()
    save = lambda i: pltpu.make_async_copy(sout.at[i], out.at[:, i, :], out_sem.at[i])
    for i in range(rows):
        centre = f1[i + 3]
        state = su0[i]
        th = jnp.tanh(state)
        sout[i] = (
            (state - sub[i])
            + step_rows(centre, f1[i + 4], f1[i + 2], coefs)
            + (1.0 - th * th) * mix_rows(wide, centre)
        )
        save(i).start()
    for i in range(rows):
        save(i).wait()


def shards(
    initial, background, mixing, diffusion, advection, obs_values, obs_weight,
    interp_weights, stencil_index, station_tile, counts,
):
    num_fields, num_levels, rows, cols = initial.shape
    chans = num_fields * num_levels
    tiles = lax.axis_size("gx")
    held = obs_values.shape[1]
    most = max(2, held * 3 // (2 * tiles))
    cap = -(-most // 8) * 8
    slots = tiles * cap
    u0 = initial.reshape(chans, rows, cols)
    ub = background.reshape(chans, rows, cols)
    f32, i32 = jnp.float32, jnp.int32
    anyspace = pl.BlockSpec(memory_space=pl.ANY)
    vmem = pl.BlockSpec(memory_space=pltpu.VMEM)
    smem = pl.BlockSpec(memory_space=pltpu.SMEM)
    dma = pltpu.SemaphoreType.DMA
    limit = 60 * 1024 * 1024
    shape = jax.ShapeDtypeStruct
    q1, mine, near, coef, mixing_t = pl.pallas_call(
        functools.partial(forward_kernel, tiles, cap),
        out_shape=(
            shape((rows + 2, chans, cols), f32),
            shape((16, slots), f32),
            shape((2, 16, slots), f32),
            shape((chans, 128), f32),
            shape((chans, chans), f32),
        ),
        in_specs=[vmem] * 5 + [smem] + [vmem] * 3 + [anyspace],
        out_specs=(anyspace, vmem, vmem, vmem, vmem),
        scratch_shapes=[
            pltpu.VMEM((tiles, cap, 128), f32),
            pltpu.VMEM((tiles, cap, 128), f32),
            pltpu.VMEM((rows + 4, chans, cols), f32),
            pltpu.VMEM((rows + 2, chans, cols), f32),
            pltpu.VMEM((rows, chans, cols), f32),
            pltpu.VMEM((rows + 2, chans, cols), f32),
            pltpu.VMEM((3, slots, slots), jnp.bfloat16),
            pltpu.VMEM((2, 16, slots), f32),
            dma((rows,)),
            dma((rows + 2,)),
            dma((tiles,)),
            dma((tiles,)),
            dma((4,)),
            dma((4,)),
            dma((2,)),
            dma((2,)),
        ],
        compiler_params=pltpu.CompilerParams(
            collective_id=0, has_side_effects=True, vmem_limit_bytes=limit),
    )(obs_values, obs_weight, interp_weights, stencil_index,
      station_tile.reshape(1, held), counts, diffusion.T, advection.transpose(0, 2, 1),
      mixing, u0)
    gradient = pl.pallas_call(
        functools.partial(adjoint_kernel, tiles),
        out_shape=shape((chans, rows, cols), f32),
        in_specs=[anyspace, anyspace, anyspace, vmem, vmem, vmem, vmem],
        out_specs=anyspace,
        scratch_shapes=[
            pltpu.VMEM((rows, chans, cols), f32),
            pltpu.VMEM((rows, chans, cols), f32),
            pltpu.VMEM((rows + 2, chans, cols), f32),
            pltpu.VMEM((rows + 6, chans, cols), f32),
            pltpu.VMEM((rows + 6, chans, cols), f32),
            pltpu.VMEM((rows, chans, cols), f32),
            pltpu.VMEM((4, 128, WIN), f32),
            pltpu.VMEM((3, 8, slots), i32),
            pltpu.SMEM((3, 8, slots), i32),
            dma((3, rows + 2)),
            dma,
            dma((rows,)),
        ],
        compiler_params=pltpu.CompilerParams(vmem_limit_bytes=limit),
    )(u0, ub, q1, mine, near, mixing_t, coef)
    return gradient.reshape(num_fields, num_levels, rows, cols)


def solution(mesh):
    placed = (
        P("groups", None, "gx", None),
        P("groups", None, "gx", None),
        P(),
        P(),
        P(),
        P("groups", "gx"),
        P("groups", "gx"),
        P("groups", "gx"),
        P("groups", "gx"),
        P("gx", "groups"),
        P("groups", "gx"),
    )
    return jax.shard_map(
        shards, mesh=mesh, in_specs=placed, out_specs=P("groups", None, "gx", None), check_vma=False
    )
```

```python
import functools
import jax
import jax.numpy as jnp
from jax import lax
from jax.experimental import pallas as pl
from jax.experimental.pallas import tpu as pltpu
from jax.sharding import PartitionSpec as P

MESH = pl.DeviceIdType.MESH
WIN = 256


def fdot(a, b, dims):
    return lax.dot_general(a, b, (dims, ((), ())), preferred_element_type=jnp.float32)


def split3(v):
    hi = v.astype(jnp.bfloat16)
    rest = v - hi.astype(jnp.float32)
    mid = rest.astype(jnp.bfloat16)
    lo = (rest - mid.astype(jnp.float32)).astype(jnp.bfloat16)
    return hi, mid, lo


def widen_mix(m):
    hi = m.astype(jnp.bfloat16)
    lo = (m - hi.astype(jnp.float32)).astype(jnp.bfloat16)
    return jnp.concatenate([hi, hi, lo], axis=1)


def mix_rows(wide, v):
    hi = v.astype(jnp.bfloat16).astype(jnp.float32)
    parts = jnp.concatenate([hi, v - hi, hi], axis=0).astype(jnp.bfloat16)
    return fdot(wide, parts, ((1,), (0,)))


def shifts(v):
    cols = v.shape[1]
    lane = lax.broadcasted_iota(jnp.int32, (v.shape[0], 128), 1)
    east, west = pltpu.roll(v, cols - 1, 1), pltpu.roll(v, 1, 1)
    last = jnp.where(lane == 127, 0.0, east[:, cols - 128:])
    start = jnp.where(lane == 0, 0.0, west[:, :128])
    east = jnp.concatenate([east[:, :cols - 128], last], axis=1)
    west = jnp.concatenate([start, west[:, 128:]], axis=1)
    return east, west


def step_rows(centre, above, below, coef):
    east, west = shifts(centre)
    return (
        coef[0] * centre + coef[1] * above + coef[2] * below + coef[3] * east + coef[4] * west
    )


def exact_dot(hot, v, dims):
    hi, mid, lo = split3(v)
    return fdot(hot, hi, dims) + fdot(hot, mid, dims) + fdot(hot, lo, dims)


def hot_of(condition):
    return condition.astype(jnp.float32).astype(jnp.bfloat16)


def coef_columns(coef_ref, sign):
    c, a, b = coef_ref[:, 0:1], sign * coef_ref[:, 1:2], sign * coef_ref[:, 2:3]
    return 1.0 - 4.0 * c, c + a, c - a, c + b, c - b


def channel_column(table, chans):
    levels, fields = table.shape
    row = lax.broadcasted_iota(jnp.int32, (chans, fields), 0)
    field = lax.broadcasted_iota(jnp.int32, (chans, fields), 1)
    total = None
    for level in range(levels):
        hot = hot_of(row == field * levels + level)
        part = exact_dot(hot, table, ((1,), (1,)))[:, level:level + 1]
        total = part if total is None else total + part
    return total


def window_weights(column, weights, cols):
    block = jnp.minimum(jnp.floor(column * (1.0 / 128)), float(cols // 128 - 2))
    local = column - 128.0 * block
    lane = lax.broadcasted_iota(jnp.int32, (column.shape[0], WIN), 1).astype(jnp.float32)
    left, right = lane == local, lane == local + 1.0
    top = jnp.where(left, weights[0], 0.0) + jnp.where(right, weights[1], 0.0)
    low = jnp.where(left, weights[2], 0.0) + jnp.where(right, weights[3], 0.0)
    return top, low


def split_cell(cell, rows, cols):
    chan = jnp.floor(cell * (1.0 / (rows * cols)))
    rest = cell - chan * (rows * cols)
    line = jnp.floor(rest * (1.0 / cols))
    return line, chan, rest - line * cols


def place_rows(line, chan, column, count, cols):
    block = jnp.minimum(jnp.floor(column * (1.0 / 128)), float(cols // 128 - 2)) * 128.0
    zero = jnp.zeros_like(line)
    return jnp.concatenate([line, chan, block, count] + [zero] * 4, axis=0).astype(jnp.int32)


def forward_kernel(
    tiles, cap, vals, wts, interp, cells, target, count, diffusion, advection, mixing, u0,
    q1, mine, near, coef_out, mixing_t,
    send, recv, su0, su1, su2, sq1, hots, outbox,
    in_sem, out_sem, send_sem, recv_sem, halo_send, halo_recv, near_send, near_recv,
):
    me = lax.axis_index("gx")
    chans, rows, cols = u0.shape
    held = target.shape[1]
    slots = tiles * cap
    nt = ((1,), (1,))
    loads = [
        pltpu.make_async_copy(u0.at[:, r, :], su0.at[r + 2], in_sem.at[r]) for r in range(rows)
    ]
    for copy in loads:
        copy.start()
    barrier = pltpu.get_barrier_semaphore()

    def greet(d, _):
        pl.semaphore_signal(
            barrier, inc=1, device_id={"gx": lax.rem(me + d, tiles)}, device_id_type=MESH
        )
        return 0

    lax.fori_loop(1, tiles, greet, 0)
    names = target[...]
    match = (lax.broadcasted_iota(jnp.int32, (tiles, held), 0) == names).astype(jnp.float32)
    before = hot_of(
        lax.broadcasted_iota(jnp.int32, (held, held), 0)
        < lax.broadcasted_iota(jnp.int32, (held, held), 1)
    )
    ranks = fdot(match.astype(jnp.bfloat16), before, ((1,), (0,)))
    rank = jnp.sum(match * ranks, axis=0, keepdims=True).astype(jnp.int32)
    position = names * cap + rank
    hot = hot_of(lax.broadcasted_iota(jnp.int32, (slots, held), 0) == position)
    live = lax.broadcasted_iota(jnp.int32, (1, held), 1) < count[0, 0]
    weight = jnp.where(live, wts[...], 0.0)
    recs = jnp.concatenate(
        [vals[...], weight, interp[...], cells[0:1, :].astype(jnp.float32),
         jnp.zeros((120, held), jnp.float32)], axis=0)
    send[...] = exact_dot(hot, recs, nt).reshape(tiles, cap, 128)
    pl.semaphore_wait(barrier, tiles - 1)

    def edge(up, k):
        if up:
            src, dst, at, to = rows - 2 + k, k, k, me + 1
        else:
            src, dst, at, to = k, rows + 2 + k, 2 + k, me - 1
        return pltpu.make_async_remote_copy(
            src_ref=u0.at[:, src, :], dst_ref=su0.at[dst],
            send_sem=halo_send.at[at], recv_sem=halo_recv.at[at],
            device_id={"gx": to}, device_id_type=MESH)

    def parcel(d, to, row):
        return pltpu.make_async_remote_copy(
            src_ref=send.at[to], dst_ref=recv.at[row],
            send_sem=send_sem.at[d], recv_sem=recv_sem.at[d],
            device_id={"gx": to}, device_id_type=MESH)

    def start(d, _):
        parcel(d, lax.rem(me + d, tiles), me).start()
        return 0

    def finish(d, _):
        parcel(d, lax.rem(me + d, tiles), me).wait_send()
        source = lax.rem(me + tiles - d, tiles)
        parcel(d, source, source).wait_recv()
        return 0

    lax.fori_loop(1, tiles, start, 0)

    @pl.when(me < tiles - 1)
    def _():
        edge(True, 1).start()
        edge(True, 0).start()

    @pl.when(me > 0)
    def _():
        edge(False, 0).start()
        edge(False, 1).start()

    recv[me] = send[me]
    columns = [channel_column(t, chans) for t in (diffusion[...], advection[0], advection[1])]
    lane = lax.broadcasted_iota(jnp.int32, (chans, 128), 1)
    coef_out[...] = jnp.where(
        lane == 0, columns[0], jnp.where(lane == 1, columns[1], columns[2]))
    mixing_t[...] = mixing[...].T
    wide = widen_mix(mixing[...])
    coefs = coef_columns(coef_out, 1.0)

    def first(i, _):
        centre = su0[i + 1]
        su1[i] = step_rows(centre, su0[i + 2], su0[i], coefs) + mix_rows(wide, jnp.tanh(centre))
        return 0

    for copy in loads:
        copy.wait()
    lax.fori_loop(2, rows, first, 0, unroll=2)

    lax.fori_loop(1, tiles, finish, 0)
    records = recv[...].reshape(slots, 128)
    turned = records.T
    weights = turned[2:3, :]
    line, chan, column = split_cell(turned[7:8, :], rows, cols)
    ahead = hot_of(
        lax.broadcasted_iota(jnp.int32, (slots, slots), 0)
        < lax.broadcasted_iota(jnp.int32, (slots, slots), 1)
    )
    alive = (weights > 0.0).astype(jnp.float32)
    masks = jnp.concatenate(
        [alive, jnp.where(line >= rows - 3, alive, 0.0), jnp.where(line <= 1.0, alive, 0.0),
         jnp.zeros((5, slots), jnp.float32)], axis=0)
    order = fdot(masks.astype(jnp.bfloat16), ahead, ((1,), (0,)))
    spot = jnp.where(masks > 0.0, order, -1.0).astype(jnp.int32)
    totals = jnp.sum(masks, axis=1, keepdims=True)
    slot = lax.broadcasted_iota(jnp.int32, (slots, slots), 0)
    for k in range(3):
        hots[k] = hot_of(slot == spot[k:k + 1, :])

    @pl.when(me < tiles - 1)
    def _():
        for k in range(2):
            edge(True, k).wait_send()
            edge(False, k).wait_recv()

    @pl.when(me > 0)
    def _():
        for k in range(2):
            edge(False, k).wait_send()
            edge(True, k).wait_recv()

    blank = jnp.zeros((chans, cols), jnp.float32)

    @pl.when(me == 0)
    def _():
        su0[0] = blank
        su0[1] = blank

    @pl.when(me == tiles - 1)
    def _():
        su0[rows + 2] = blank
        su0[rows + 3] = blank

    def outer(k, _):
        return first(jnp.where(k < 2, k, rows - 2 + k), 0)

    lax.fori_loop(0, 4, outer, 0)

    @pl.when(me == 0)
    def _():
        su1[0] = blank

    @pl.when(me == tiles - 1)
    def _():
        su1[rows + 1] = blank

    stores = lambda i: pltpu.make_async_copy(sq1.at[i], q1.at[i], out_sem.at[i])

    def second(i, _):
        centre = su1[i + 1]
        th = jnp.tanh(centre)
        sq1[i + 1] = 1.0 - th * th
        stores(i + 1).start()
        su2[i] = step_rows(centre, su1[i + 2], su1[i], coefs) + mix_rows(wide, th)
        return 0

    for i in (0, rows + 1):
        th = jnp.tanh(su1[i])
        sq1[i] = 1.0 - th * th
        stores(i).start()
    lax.fori_loop(0, rows, second, 0, unroll=2)
    col = lambda k: records[:, k:k + 1]
    line_c, chan_c, column_c = split_cell(col(7), rows, cols)
    span = (rows - 1) * chans
    flat = lax.broadcasted_iota(jnp.int32, (slots, span), 1).astype(jnp.float32)
    pick = hot_of(flat == line_c * chans + chan_c)
    pick = jnp.concatenate([pick, pick], axis=1)

    def picked(state, first_row, start):
        block = state[first_row:first_row + rows - 1, :, start:start + WIN].reshape(span, WIN)
        hi = block.astype(jnp.bfloat16).astype(jnp.float32)
        both = jnp.concatenate([hi, block - hi], axis=0).astype(jnp.bfloat16)
        return fdot(pick, both, ((1,), (0,)))

    samples = [jnp.zeros((slots, 1), jnp.float32)] * 2
    lane = lax.broadcasted_iota(jnp.int32, (slots, WIN), 1).astype(jnp.float32)
    for start in range(0, cols, WIN):
        local = column_c - float(start)
        left, right = lane == local, lane == local + 1.0
        top = jnp.where(left, col(3), jnp.where(right, col(4), 0.0))
        low = jnp.where(left, col(5), jnp.where(right, col(6), 0.0))
        for which, (state, base) in enumerate(((su1, 1), (su2, 0))):
            found = picked(state, base, start) * top + picked(state, base + 1, start) * low
            samples[which] = samples[which] + jnp.sum(found, axis=1, keepdims=True)
    results = [col(2) * (samples[k] - col(k)) for k in range(2)]
    lane = lax.broadcasted_iota(jnp.int32, records.shape, 1)
    merged = jnp.where(lane == 0, results[0], jnp.where(lane == 1, results[1], 0.0)).T
    zero = jnp.zeros((7, slots), jnp.float32)
    for k, moved in ((1, -rows), (2, rows), (0, 0)):
        fields = jnp.concatenate(
            [merged[0:2, :], line + float(moved), turned[3:7, :], chan, column, zero], axis=0)
        hi, mid, lo = split3(fields)
        packed = fdot(hi, hots[k], nt) + fdot(mid, hots[k], nt) + fdot(lo, hots[k], nt)
        field = lax.broadcasted_iota(jnp.int32, packed.shape, 0)
        packed = jnp.where(field == 9, totals[k:k + 1, :], packed)
        if k == 0:
            mine[...] = packed
        else:
            outbox[k - 1] = packed

    def note(k):
        return pltpu.make_async_remote_copy(
            src_ref=outbox.at[k], dst_ref=near.at[k],
            send_sem=near_send.at[k], recv_sem=near_recv.at[k],
            device_id={"gx": me + 1 if k == 0 else me - 1}, device_id_type=MESH)

    @pl.when(me < tiles - 1)
    def _():
        note(0).start()

    @pl.when(me > 0)
    def _():
        note(1).start()

    for i in range(rows + 2):
        stores(i).wait()

    @pl.when(me == 0)
    def _():
        near[0] = jnp.zeros((16, slots), jnp.float32)

    @pl.when(me == tiles - 1)
    def _():
        near[1] = jnp.zeros((16, slots), jnp.float32)

    @pl.when(me < tiles - 1)
    def _():
        note(0).wait_send()
        note(1).wait_recv()

    @pl.when(me > 0)
    def _():
        note(1).wait_send()
        note(0).wait_recv()


def adjoint_kernel(
    tiles, u0, ub, q1, mine, near, mixing_t, coef, out,
    su0, sub, sq1, f1, f2, sout, parts, place_v, place_s, in_sem, place_sem, out_sem,
):
    me = lax.axis_index("gx")
    chans, rows, cols = u0.shape
    slots = mine.shape[1]
    load_q = [pltpu.make_async_copy(q1.at[i], sq1.at[i], in_sem.at[0, i]) for i in range(rows + 2)]
    load_u = [pltpu.make_async_copy(u0.at[:, i, :], su0.at[i], in_sem.at[1, i]) for i in range(rows)]
    load_b = [pltpu.make_async_copy(ub.at[:, i, :], sub.at[i], in_sem.at[2, i]) for i in range(rows)]
    lists = [mine[...], near[0], near[1]]
    for group, block in enumerate(lists):
        place_v[group] = place_rows(
            block[2:3, :] + 3.0, block[7:8, :], block[8:9, :], block[9:10, :], cols)
    placing = pltpu.make_async_copy(place_v, place_s, place_sem)
    placing.start()
    for copy in load_q + load_u + load_b:
        copy.start()

    def clear(i, _):
        f1[i] = jnp.zeros((chans, cols), jnp.float32)
        f2[i] = jnp.zeros((chans, cols), jnp.float32)
        return 0

    lax.fori_loop(0, rows + 6, clear, 0)
    placing.wait()
    for group in range(3):
        amount = place_s[group, 3, 0]
        for start in range(0, slots, 128):

            @pl.when(amount > start)
            def _():
                block = (mine if group == 0 else near.at[group - 1])[:, start:start + 128]
                full = jnp.concatenate([block, jnp.zeros((112, 128), jnp.float32)], axis=0).T
                col = lambda k: full[:, k:k + 1]
                top, low = window_weights(col(8), [col(3 + k) for k in range(4)], cols)
                parts[0] = col(0) * top
                parts[1] = col(0) * low
                parts[2] = col(1) * top
                parts[3] = col(1) * low

                def add(j2, _):
                    for k in range(2):
                        j = j2 * 2 + k
                        at, ch = place_s[group, 0, start + j], place_s[group, 1, start + j]
                        block = pl.multiple_of(place_s[group, 2, start + j], 128)
                        spots = [
                            (ref, (at + step, pl.ds(ch, 1), pl.ds(block, WIN)), 2 * t + step)
                            for t, ref in enumerate((f1, f2)) for step in range(2)]
                        sums = [
                            ref[spot] + parts[part, pl.ds(j, 1), :] for ref, spot, part in spots]
                        for (ref, spot, _), total in zip(spots, sums):
                            ref[spot] = total
                    return 0

                lax.fori_loop(0, (jnp.minimum(amount - start, 128) + 1) // 2, add, 0)

    wide = widen_mix(mixing_t[...])
    coefs = coef_columns(coef, -1.0)
    for copy in load_q:
        copy.wait()

    def first(i, _):
        centre = f2[i + 2]
        spread = step_rows(centre, f2[i + 3], f2[i + 1], coefs)
        f1[i + 2] = f1[i + 2] + spread + sq1[i] * mix_rows(wide, centre)
        return 0

    lax.fori_loop(0, rows + 2, first, 0, unroll=2)

    @pl.when(me == 0)
    def _():
        f1[2] = jnp.zeros((chans, cols), jnp.float32)

    @pl.when(me == tiles - 1)
    def _():
        f1[rows + 3] = jnp.zeros((chans, cols), jnp.float32)

    for copy in load_u + load_b:
        copy.wait()
    save = lambda i: pltpu.make_async_copy(sout.at[i], out.at[:, i, :], out_sem.at[i])
    for i in range(rows):
        centre = f1[i + 3]
        state = su0[i]
        th = jnp.tanh(state)
        sout[i] = (
            (state - sub[i])
            + step_rows(centre, f1[i + 4], f1[i + 2], coefs)
            + (1.0 - th * th) * mix_rows(wide, centre)
        )
        save(i).start()
    for i in range(rows):
        save(i).wait()


def shards(
    initial, background, mixing, diffusion, advection, obs_values, obs_weight,
    interp_weights, stencil_index, station_tile, counts,
):
    num_fields, num_levels, rows, cols = initial.shape
    chans = num_fields * num_levels
    tiles = lax.axis_size("gx")
    held = obs_values.shape[1]
    most = max(2, held * 3 // (2 * tiles))
    cap = -(-most // 8) * 8
    slots = tiles * cap
    u0 = initial.reshape(chans, rows, cols)
    ub = background.reshape(chans, rows, cols)
    f32, i32 = jnp.float32, jnp.int32
    anyspace = pl.BlockSpec(memory_space=pl.ANY)
    vmem = pl.BlockSpec(memory_space=pltpu.VMEM)
    smem = pl.BlockSpec(memory_space=pltpu.SMEM)
    dma = pltpu.SemaphoreType.DMA
    limit = 60 * 1024 * 1024
    shape = jax.ShapeDtypeStruct
    q1, mine, near, coef, mixing_t = pl.pallas_call(
        functools.partial(forward_kernel, tiles, cap),
        out_shape=(
            shape((rows + 2, chans, cols), f32),
            shape((16, slots), f32),
            shape((2, 16, slots), f32),
            shape((chans, 128), f32),
            shape((chans, chans), f32),
        ),
        in_specs=[vmem] * 5 + [smem] + [vmem] * 3 + [anyspace],
        out_specs=(anyspace, vmem, vmem, vmem, vmem),
        scratch_shapes=[
            pltpu.VMEM((tiles, cap, 128), f32),
            pltpu.VMEM((tiles, cap, 128), f32),
            pltpu.VMEM((rows + 4, chans, cols), f32),
            pltpu.VMEM((rows + 2, chans, cols), f32),
            pltpu.VMEM((rows, chans, cols), f32),
            pltpu.VMEM((rows + 2, chans, cols), f32),
            pltpu.VMEM((3, slots, slots), jnp.bfloat16),
            pltpu.VMEM((2, 16, slots), f32),
            dma((rows,)),
            dma((rows + 2,)),
            dma((tiles,)),
            dma((tiles,)),
            dma((4,)),
            dma((4,)),
            dma((2,)),
            dma((2,)),
        ],
        compiler_params=pltpu.CompilerParams(
            collective_id=0, has_side_effects=True, vmem_limit_bytes=limit),
    )(obs_values, obs_weight, interp_weights, stencil_index,
      station_tile.reshape(1, held), counts, diffusion.T, advection.transpose(0, 2, 1),
      mixing, u0)
    gradient = pl.pallas_call(
        functools.partial(adjoint_kernel, tiles),
        out_shape=shape((chans, rows, cols), f32),
        in_specs=[anyspace, anyspace, anyspace, vmem, vmem, vmem, vmem],
        out_specs=anyspace,
        scratch_shapes=[
            pltpu.VMEM((rows, chans, cols), f32),
            pltpu.VMEM((rows, chans, cols), f32),
            pltpu.VMEM((rows + 2, chans, cols), f32),
            pltpu.VMEM((rows + 6, chans, cols), f32),
            pltpu.VMEM((rows + 6, chans, cols), f32),
            pltpu.VMEM((rows, chans, cols), f32),
            pltpu.VMEM((4, 128, WIN), f32),
            pltpu.VMEM((3, 8, slots), i32),
            pltpu.SMEM((3, 8, slots), i32),
            dma((3, rows + 2)),
            dma,
            dma((rows,)),
        ],
        compiler_params=pltpu.CompilerParams(vmem_limit_bytes=limit),
    )(u0, ub, q1, mine, near, mixing_t, coef)
    return gradient.reshape(num_fields, num_levels, rows, cols)


def solution(mesh):
    placed = (
        P("groups", None, "gx", None),
        P("groups", None, "gx", None),
        P(),
        P(),
        P(),
        P("groups", "gx"),
        P("groups", "gx"),
        P("groups", "gx"),
        P("groups", "gx"),
        P("gx", "groups"),
        P("groups", "gx"),
    )
    return jax.shard_map(
        shards, mesh=mesh, in_specs=placed, out_specs=P("groups", None, "gx", None), check_vma=False
    )
```
